32 devices in a mesh: groups: 2 (over y), seq: 8 (over z, x), tensor: 2 (over core).
Axes of the slice: x: 2, y: 2, z: 4, core: 2. Of those that a mesh axis runs over, the one named last changes fastest.
Arguments:
- queries: bfloat16 [4, 1024, 2048], P(('groups', 'tensor'), 'seq'), parts along dimension 0, may hold values from -33 to 33
- keys: bfloat16 [4, 1024, 2048], P(('groups', 'tensor'), 'seq'), parts along dimension 0, may hold values from -33 to 33
- values: bfloat16 [4, 1024, 2048], P(('groups', 'tensor'), 'seq'), parts along dimension 0, may hold values from -6 to 6
- out_grad: bfloat16 [4, 1024, 2048], P(('groups', 'tensor'), 'seq'), parts along dimension 0, may hold values from -96 to 96
- tile_lists: int32 [32, 12], P(('groups', 'tensor')), parts along dimension 0, may hold values from -1 to 15, as said below
Outputs:
- query_grad: bfloat16 [4, 1024, 2048], P(('groups', 'tensor'), 'seq'), parts along dimension 0
- key_grad: bfloat16 [4, 1024, 2048], P(('groups', 'tensor'), 'seq'), parts along dimension 0
- value_grad: bfloat16 [4, 1024, 2048], P(('groups', 'tensor'), 'seq'), parts along dimension 0
The draws below stay inside these ranges and needn't reach their ends.
There are 2 independent parts, one for each index of `groups`. The reference program is written for one: setup_inputs(seed, part) draws one part's arguments, and reference() takes and returns one part's arrays. A program takes and returns all parts, laid end to end along the dimension named above; each array names one. Nothing has to cross between parts.
Inputs may be any that keep to these rules, and one draw needn't show every extreme that they name: `tile_lists`: row i begins with i; its other entries are distinct tiles within 8 of i, followed by -1 entries only where fewer such tiles lie inside the clip.
All inputs are finite; a program needn't handle non-finite values.
Results may differ from the reference program's by a relative error of at most 0.012.
Values may be sent and summed in bfloat16 or wider, within the bound.
A program may use at most 128 MiB of HBM per device.

```python
import math
import jax
import jax.numpy as jnp
from jax import lax

DH = 128
TILE = 128
RADIUS = 8
WIN = 12
HD = 2048
SEGS = 2
SEG = 1024
TILES = 16


def drawn_pair(key):
    key = jax.random.fold_in(key, 11)
    first, second = jax.random.split(key, 2)
    token_count = SEGS * SEG
    base_query = jnp.clip(jax.random.normal(first, (token_count, HD), jnp.float32), -6.0, 6.0)
    base_key = jnp.clip(jax.random.normal(second, (token_count, HD), jnp.float32), -6.0, 6.0)
    key_rows = base_key
    query_rows = base_query
    return (query_rows.reshape(SEGS, SEG, HD), key_rows.reshape(SEGS, SEG, HD))


def draw_queries(key, part):
    return drawn_pair(key)[0].astype(jnp.bfloat16)


def draw_keys(key, part):
    return drawn_pair(key)[1].astype(jnp.bfloat16)


def draw_tile_lists(key, part):
    key = jax.random.fold_in(key, 23)
    offsets = jnp.concatenate([jnp.arange(-RADIUS, 0, dtype=jnp.int32), jnp.arange(1, RADIUS + 1, dtype=jnp.int32)])
    ranking = jax.random.randint(key, (TILES, 2 * RADIUS), 0, 1 << 20, dtype=jnp.int32)
    here = jnp.arange(TILES, dtype=jnp.int32)[:, None]
    target = here + offsets[None, :]
    inside = jnp.logical_and(target >= 0, target < TILES)
    ordering = (1 - inside.astype(jnp.int32)) * (1 << 25) + ranking * 32 + jnp.arange(2 * RADIUS, dtype=jnp.int32)[None, :]
    order = jnp.argsort(ordering, axis=1)[:, :WIN - 1]
    chosen = jnp.take_along_axis(target, order, axis=1)
    chosen_inside = jnp.take_along_axis(inside, order, axis=1)
    chosen = jnp.where(chosen_inside, chosen, -1)
    return jnp.concatenate([here, chosen], 1).astype(jnp.int32)


def block_levels(key, dims, cuts, smallest, top_value):
    def one(dim, blocks):
        heights = jax.random.uniform(jax.random.fold_in(jax.random.fold_in(key, 6), dim), (blocks,), jnp.float32, smallest / len(cuts), top_value / len(cuts))
        return jnp.repeat(jnp.exp(heights), dims[dim] // blocks).reshape((-1,) + (1,) * (len(dims) - dim - 1))

    level = one(*cuts[0])
    for cut in cuts[1:]:
        level = level * one(*cut)
    return level


def centred(stream_key, extent, width, limit, pieces=(), held_as=jnp.bfloat16):
    values = width * jax.random.normal(stream_key, extent, jnp.float32)
    if pieces:
        values = values * block_levels(stream_key, extent, pieces, -0.22, 0.18)
    return jnp.clip(values, -limit, limit).astype(held_as)


def setup_inputs(seed: int = 0, part: int = 0) -> dict:
    seeds = jax.random.split(jax.random.key(seed), 6)
    own_keys = jax.random.split(jax.random.fold_in(seeds[5], part), 6)
    return {
        "queries": draw_queries(jax.random.fold_in(jax.random.fold_in(seeds[5], part), 71), part),
        "keys": draw_keys(jax.random.fold_in(jax.random.fold_in(seeds[5], part), 71), part),
        "values": centred(own_keys[2], (SEGS, SEG, HD), 1.0, 6.0, ((0, 2), (1, 8))),
        "out_grad": centred(own_keys[3], (SEGS, SEG, HD), 16.0, 96.0, ((0, 2), (1, 8))),
        "tile_lists": draw_tile_lists(jax.random.fold_in(jax.random.fold_in(seeds[5], part), 71), part),
    }


def reference(queries, keys, values, out_grad, tile_lists):
    token_count = queries.shape[0] * queries.shape[1]
    feature_count = queries.shape[2]
    head_count = feature_count // DH
    tile_count = token_count // TILE
    score_scale = 1.0 / math.sqrt(DH)

    def per_head(head):

        def head_tiles(array):
            rows = array.reshape(token_count, feature_count)
            return lax.dynamic_slice_in_dim(rows, head * DH, DH, 1).reshape(tile_count, TILE, DH)
        q_tiles = head_tiles(queries)
        k_tiles = head_tiles(keys)
        v_tiles = head_tiles(values)
        g_tiles = head_tiles(out_grad)

        def step(totals, tile_index):
            key_total, value_total = totals
            tile_row = tile_lists[tile_index]
            present = tile_row >= 0
            local_tile = jnp.maximum(tile_row, 0).astype(jnp.int32)
            key_rows = k_tiles[local_tile].reshape(WIN * TILE, DH)
            value_rows = v_tiles[local_tile].reshape(WIN * TILE, DH)
            query_rows = q_tiles[tile_index]
            grad_rows = g_tiles[tile_index]
            scores = jnp.dot(query_rows, key_rows.T, preferred_element_type=jnp.float32) * score_scale
            live_keys = jnp.repeat(present, TILE)
            scores = jnp.where(live_keys[None, :], scores, -1e+30)
            row_max = lax.optimization_barrier(jnp.max(scores, axis=1, keepdims=True))
            weights = jnp.exp(scores - row_max)
            weights = weights / lax.optimization_barrier(jnp.sum(weights, axis=1, keepdims=True))
            weights_b = weights.astype(jnp.bfloat16)
            recomputed = jnp.dot(weights_b, value_rows, preferred_element_type=jnp.float32)
            delta = lax.optimization_barrier(jnp.sum(grad_rows.astype(jnp.float32) * recomputed, axis=1, keepdims=True))
            prob_grad = jnp.dot(grad_rows, value_rows.T, preferred_element_type=jnp.float32)
            score_grad = (weights * (prob_grad - delta) * score_scale).astype(jnp.bfloat16)
            query_part = jnp.dot(score_grad, key_rows, preferred_element_type=jnp.float32).astype(jnp.bfloat16)
            key_part = jnp.dot(score_grad.T, query_rows, preferred_element_type=jnp.float32).reshape(WIN, TILE, DH)
            value_part = jnp.dot(weights_b.T, grad_rows, preferred_element_type=jnp.float32).reshape(WIN, TILE, DH)
            key_total = key_total.at[local_tile].add(key_part)
            value_total = value_total.at[local_tile].add(value_part)
            return ((key_total, value_total), query_part)
        zeros_tiles = jnp.zeros((tile_count, TILE, DH), jnp.float32)
        totals, query_parts = lax.scan(step, (zeros_tiles, zeros_tiles), jnp.arange(tile_count, dtype=jnp.int32))
        key_total, value_total = totals
        return (query_parts.reshape(token_count, DH), key_total.astype(jnp.bfloat16).reshape(token_count, DH), value_total.astype(jnp.bfloat16).reshape(token_count, DH))
    query_heads, key_heads, value_heads = lax.map(per_head, jnp.arange(head_count, dtype=jnp.int32))

    def arrange(array):
        return jnp.transpose(array, (1, 0, 2)).reshape(queries.shape)
    return (arrange(query_heads), arrange(key_heads), arrange(value_heads))
```

```python
import functools
import math

import jax
import jax.numpy as jnp
from jax import lax
from jax.experimental import pallas as pl
from jax.experimental.pallas import tpu as pltpu
from jax.sharding import PartitionSpec as P

HEADS = 16
DH = 128
TILE = 128
RADIUS = 8
WIN = 12


block_tiles = 4


def padded_2(block, sides, width):
    for axis, dim in sides:
        count = lax.axis_size(axis)
        forward = [(i, i + 1) for i in range(count - 1)]
        backward = [(target, source) for source, target in forward]
        low = lax.ppermute(
            lax.slice_in_dim(block, block.shape[dim] - width, None, axis=dim), axis, forward
        )
        high = lax.ppermute(lax.slice_in_dim(block, 0, width, axis=dim), axis, backward)
        block = jnp.concatenate([low, block, high], axis=dim)
    return block


def key_rims(key_rows, value_rows):
    joined = jnp.concatenate([key_rows, value_rows], 1)
    return padded_2(joined, (("tensor", 0),), RADIUS * TILE)


def finish_rims(grads_ext, segment, local_width):
    rim_rows = RADIUS * TILE
    outer_rows = jnp.concatenate([grads_ext[:rim_rows], grads_ext[-rim_rows:]], 0)
    arrived = padded_2(outer_rows, (("tensor", 0),), rim_rows)
    own_rows = grads_ext[rim_rows : rim_rows + segment]
    own_rows = own_rows.at[:rim_rows].add(arrived[:rim_rows])
    own_rows = own_rows.at[segment - rim_rows :].add(arrived[3 * rim_rows :])
    own_rows = own_rows.astype(jnp.bfloat16)
    return (own_rows[:, :local_width], own_rows[:, local_width:])


def regrouped_body(queries, keys, values, out_grad, tile_lists):
    span_rows = queries.shape[1]
    feature_count = queries.shape[2]
    seq_count = lax.axis_size("seq")
    heads_here = HEADS // seq_count
    local_width = heads_here * DH
    score_scale = 1.0 / math.sqrt(DH)
    query_tokens = queries.reshape(span_rows, feature_count)
    key_tokens = keys.reshape(span_rows, feature_count)
    value_tokens = values.reshape(span_rows, feature_count)
    grad_tokens = out_grad.reshape(span_rows, feature_count)
    query_rows, key_rows, value_rows, grad_rows = (
        lax.all_to_all(query_tokens, "seq", split_axis=1, concat_axis=0, tiled=True),
        lax.all_to_all(key_tokens, "seq", split_axis=1, concat_axis=0, tiled=True),
        lax.all_to_all(value_tokens, "seq", split_axis=1, concat_axis=0, tiled=True),
        lax.all_to_all(grad_tokens, "seq", split_axis=1, concat_axis=0, tiled=True),
    )
    padded = key_rims(key_rows, value_rows)
    segment = query_rows.shape[0]
    seg_tiles = segment // TILE
    ext_tiles = seg_tiles + 2 * RADIUS
    block_count = seg_tiles // block_tiles
    first_tile = lax.axis_index("tensor") * seg_tiles - RADIUS
    kv_tiles = padded.reshape(ext_tiles, TILE, 2 * local_width)
    query_blocks = query_rows.reshape(block_count, block_tiles, TILE, heads_here, DH)
    grad_blocks = grad_rows.reshape(block_count, block_tiles, TILE, heads_here, DH)
    list_blocks = tile_lists.reshape(block_count, block_tiles, WIN)

    def attend_block(totals, inputs):
        query_block, grad_block, tile_rows = inputs
        present = tile_rows >= 0
        local_tile = jnp.clip(tile_rows - first_tile, 0, ext_tiles - 1)
        picked = jnp.concatenate(
            [
                lax.dynamic_slice_in_dim(kv_tiles, local_tile[row, entry], 1, 0)
                for row in range(block_tiles)
                for entry in range(WIN)
            ],
            0,
        ).reshape(block_tiles, WIN * TILE, 2, heads_here, DH)
        key_sel = picked[:, :, 0]
        value_sel = picked[:, :, 1]
        scores = (
            jnp.einsum("gthd,gkhd->ghtk", query_block, key_sel, preferred_element_type=jnp.float32)
            * score_scale
        )
        live_keys = jnp.repeat(present, TILE, axis=1)
        scores = jnp.where(live_keys[:, None, None, :], scores, -1e30)
        row_max = jnp.max(scores, axis=3, keepdims=True)
        weights = jnp.exp(scores - row_max)
        weights = weights / jnp.sum(weights, axis=3, keepdims=True)
        weights_b = weights.astype(jnp.bfloat16)
        recomputed = jnp.einsum(
            "ghtk,gkhd->gthd", weights_b, value_sel, preferred_element_type=jnp.float32
        )
        delta = jnp.sum(grad_block.astype(jnp.float32) * recomputed, axis=3)
        prob_grad = jnp.einsum(
            "gthd,gkhd->ghtk", grad_block, value_sel, preferred_element_type=jnp.float32
        )
        score_grad = (
            weights * (prob_grad - jnp.transpose(delta, (0, 2, 1))[..., None]) * score_scale
        ).astype(jnp.bfloat16)
        query_part = jnp.einsum(
            "ghtk,gkhd->gthd", score_grad, key_sel, preferred_element_type=jnp.float32
        ).astype(jnp.bfloat16)
        key_part = jnp.einsum(
            "ghtk,gthd->gkhd", score_grad, query_block, preferred_element_type=jnp.float32
        )
        value_part = jnp.einsum(
            "ghtk,gthd->gkhd", weights_b, grad_block, preferred_element_type=jnp.float32
        )
        key_terms = jnp.concatenate([key_part, value_part], 2).reshape(
            block_tiles, WIN, TILE, 2 * local_width
        )
        totals = totals.at[local_tile].add(key_terms)
        return (totals, query_part)

    initial = jnp.zeros((ext_tiles, TILE, 2 * local_width), jnp.float32)
    grads_ext, query_parts = lax.scan(
        attend_block, initial, (query_blocks, grad_blocks, list_blocks)
    )
    query_grad = query_parts.reshape(segment, local_width)
    grads_ext = grads_ext.reshape(ext_tiles * TILE, 2 * local_width)
    query_back = lax.all_to_all(query_grad, "seq", split_axis=0, concat_axis=1, tiled=True)
    key_grad, value_grad = finish_rims(grads_ext, segment, local_width)
    key_back, value_back = (
        lax.all_to_all(key_grad, "seq", split_axis=0, concat_axis=1, tiled=True),
        lax.all_to_all(value_grad, "seq", split_axis=0, concat_axis=1, tiled=True),
    )
    out_shape = queries.shape
    return (
        query_back.reshape(out_shape),
        key_back.reshape(out_shape),
        value_back.reshape(out_shape),
    )


SEQ_DEVICES = 8
TENSOR_DEVICES = 2
SIDE_TILES = 8
CHIPS = 4
INNER_SLOTS = 3
MAX_STEPS = INNER_SLOTS * CHIPS
RELAY_AHEAD = 6


def half_kernel(
    q_hbm,
    k_hbm,
    v_hbm,
    g_hbm,
    lists_hbm,
    grads,
    staged,
    qg,
    kv,
    lists_all,
    bias,
    key_t,
    expo,
    prob_grad,
    stat_out,
    stat_in,
    dv_sum,
    dk_sum,
    dq_keep,
    part_out,
    part_in,
    dq_out,
    dkv_out,
    in_send,
    in_recv,
    relay_send,
    relay_recv,
    stat_send,
    stat_recv,
    part_send,
    part_recv,
    out_send,
    out_recv,
    list_send,
    list_recv,
    local_sem,
):
    seq_here = lax.axis_index("seq")
    core = lax.axis_index("tensor")
    z_here = seq_here // 2
    x_here = lax.rem(seq_here, 2)
    side = z_here // 2
    row = z_here + side * (3 - 2 * z_here)
    steps = CHIPS * (1 + 2 * row)
    score_scale = 1.0 / math.sqrt(DH)

    def seq_of(row_there, x_there, side_there):
        return 2 * (row_there + side_there * (3 - 2 * row_there)) + x_there

    def chip_at(reach):
        row_there = lax.rem(row + reach // 2, 2)
        x_there = lax.rem(x_here + reach % 2, 2)
        return row_there, x_there

    def head_of(slot):
        return row * 4 * slot + (1 - row) * 4 * INNER_SLOTS + 2 * x_here + core

    mirror = (seq_of(row, x_here, 1 - side), core)

    def columns(index):
        return pl.ds(pl.multiple_of(index * DH, DH), DH)

    def remote(src, dst, send, recv, there):
        return pltpu.make_async_remote_copy(
            src_ref=src,
            dst_ref=dst,
            send_sem=send,
            recv_sem=recv,
            device_id={"seq": there[0], "tensor": there[1]},
            device_id_type=pl.DeviceIdType.MESH,
        )

    def settled(ref, sem):
        pltpu.make_async_copy(ref, ref, sem).wait()

    staging = [
        pltpu.make_async_copy(src, staged.at[which], local_sem.at[which])
        for which, src in enumerate((q_hbm, g_hbm, k_hbm, v_hbm))
    ]
    for copy in staging:
        copy.start()
    own_list = pltpu.make_async_copy(lists_hbm, lists_all.at[core], local_sem.at[4])
    own_list.start()

    barrier = pltpu.get_barrier_semaphore()
    greeted = [mirror]
    for reach in range(CHIPS):
        row_there, x_there = chip_at(reach)
        for turn in range(2):
            if reach or turn:
                greeted.append((seq_of(row_there, x_there, side), lax.rem(core + turn, 2)))
    for there in greeted:
        pl.semaphore_signal(
            barrier,
            inc=1,
            device_id={"seq": there[0], "tensor": there[1]},
            device_id_type=pl.DeviceIdType.MESH,
        )
    pl.semaphore_wait(barrier, len(greeted))

    other_core = lax.rem(core + 1, 2)
    remote(
        lists_hbm, lists_all.at[core], list_send.at[0], list_recv.at[core], (seq_here, other_core)
    ).start()

    sends = []
    for row_there, slot in ((1, 0), (0, 0), (1, 1), (1, 2)):
        for which in range(2):
            for dx in range(2):
                for dc in range(2):
                    sends.append((row_there, slot, which, dx, dc))

    def send_parts(row_there, slot, which, dx, dc):
        x_there = lax.rem(x_here + dx, 2)
        core_there = lax.rem(core + dc, 2)
        head = (4 * slot if row_there else 4 * INNER_SLOTS) + 2 * x_there + core_there
        reach = 2 * lax.rem(row + row_there, 2) + dx
        place = 2 * reach + core
        src = staged.at[pl.ds(2 * which, 2), :, columns(head)]
        dst = (kv if which else qg).at[slot, :, place]
        there = (seq_of(row_there, x_there, side), core_there)
        return src, dst, in_recv.at[which, slot, place], there

    for copy in staging[:2]:
        copy.wait()
    for index, send in enumerate(sends):
        if index == 4:
            for copy in staging[2:]:
                copy.wait()
        src, dst, recv, there = send_parts(*send)
        away = remote(src, dst, in_send.at[index], recv, there)
        if send[3] or send[4]:
            away.start()
        else:
            stays = pltpu.make_async_copy(src, dst, recv)

            @pl.when(row == send[0])
            def _():
                stays.start()

            @pl.when(row != send[0])
            def _():
                away.start()

    def relay(step):
        slot = step // CHIPS
        reach = step % CHIPS
        for turn in range(2):
            place = 2 * reach + turn
            block = qg.at[slot, :, place]
            settled(block, in_recv.at[0, slot, place])
            remote(
                block,
                qg.at[slot, :, SIDE_TILES + place],
                relay_send.at[slot, place],
                relay_recv.at[slot, place],
                mirror,
            ).start()

    for step in range(CHIPS):
        relay(step)

    @pl.when(row == 1)
    def _():
        for step in range(CHIPS, RELAY_AHEAD):
            relay(step)

    own_list.wait()
    settled(lists_all.at[other_core], list_recv.at[other_core])
    ids = lax.broadcasted_iota(jnp.int32, (SIDE_TILES, TILE), 0)
    id_row = lax.rem(row + ids // 4, 2)
    id_x = lax.rem(x_here + lax.rem(ids // 2, 2), 2)
    key_ids = 8 * lax.rem(ids, 2) + 2 * (id_row + side * (3 - 2 * id_row)) + id_x
    for chunk in range(2 * CHIPS):
        row_there, x_there = chip_at(chunk % CHIPS)
        chip = seq_of(row_there, x_there, side if chunk < CHIPS else 1 - side)
        for turn in range(2):
            listed = lists_all[turn, pl.ds(chip, 1), :]
            miss = jnp.full((SIDE_TILES, TILE), -1e30, jnp.float32)
            for entry in range(WIN):
                miss = jnp.where(listed[:, entry : entry + 1] == key_ids, 0.0, miss)
            bias[chunk, :, turn * TILE : (turn + 1) * TILE] = miss

    def turned(block):
        return block.astype(jnp.float32).T.astype(jnp.bfloat16)

    def pair_of(ref, slot, which, pair):
        return ref[slot, which, pl.ds(2 * pair, 2)].reshape(2 * TILE, DH)

    def key_rows(index):
        return slice(index * 2 * TILE, (index + 1) * 2 * TILE)

    def fold(block, op):
        return op(block.reshape(2 * TILE // 8, 8, 2 * TILE), axis=0)

    def front(step):
        slot = step // CHIPS
        reach = step % CHIPS
        buffer = step % 2

        @pl.when(reach == 0)
        def _():
            for place in range(SIDE_TILES):
                settled(kv.at[slot, :, place], in_recv.at[1, slot, place])
            for pair in range(CHIPS):
                key_t[slot, pair] = turned(pair_of(kv, slot, 0, pair))

        for far in range(2):
            chunk = CHIPS * far + reach
            if far:
                for turn in range(2):
                    place = 2 * reach + turn
                    settled(qg.at[slot, :, SIDE_TILES + place], relay_recv.at[slot, place])
            query_t = turned(pair_of(qg, slot, 0, chunk))
            grad_t = turned(pair_of(qg, slot, 1, chunk))
            top = jnp.full((8, 2 * TILE), -3e38, jnp.float32)
            for pair in range(CHIPS):
                scores = (
                    jnp.dot(pair_of(kv, slot, 0, pair), query_t, preferred_element_type=jnp.float32)
                    * score_scale
                )
                scores = jnp.concatenate(
                    [
                        scores[:TILE] + bias[chunk, 2 * pair : 2 * pair + 1, :],
                        scores[TILE:] + bias[chunk, 2 * pair + 1 : 2 * pair + 2, :],
                    ],
                    axis=0,
                )
                expo[buffer, far, key_rows(pair), :] = scores
                top = jnp.maximum(top, fold(scores, jnp.max))
            top = jnp.max(top, axis=0, keepdims=True)
            total = jnp.zeros((8, 2 * TILE), jnp.float32)
            delta = jnp.zeros((8, 2 * TILE), jnp.float32)
            for pair in range(CHIPS):
                product = jnp.dot(
                    pair_of(kv, slot, 1, pair), grad_t, preferred_element_type=jnp.float32
                )
                weights = jnp.exp(expo[buffer, far, key_rows(pair), :] - top)
                expo[buffer, far, key_rows(pair), :] = weights
                prob_grad[buffer, far, key_rows(pair), :] = product
                total = total + fold(weights, jnp.sum)
                delta = delta + fold(weights * product, jnp.sum)
            stat_out[step, far, 0:1, :] = top
            stat_out[step, far, 1:2, :] = jnp.sum(total, axis=0, keepdims=True)
            stat_out[step, far, 2:3, :] = jnp.sum(delta, axis=0, keepdims=True)
        remote(
            stat_out.at[step], stat_in.at[step], stat_send.at[step], stat_recv.at[step], mirror
        ).start()

    def back(step):
        slot = step // CHIPS
        reach = step % CHIPS
        buffer = step % 2

        @pl.when(reach == 0)
        def _():
            dv_sum[...] = jnp.zeros_like(dv_sum)
            dk_sum[...] = jnp.zeros_like(dk_sum)

        settled(stat_in.at[step], stat_recv.at[step])
        for far in (1, 0):
            chunk = CHIPS * far + reach
            query_pair = pair_of(qg, slot, 0, chunk)
            grad_pair = pair_of(qg, slot, 1, chunk)
            top = stat_out[step, far, 0:1, :]
            top_there = stat_in[step, 1 - far, 0:1, :]
            top_all = jnp.maximum(top, top_there)
            part = jnp.exp(top - top_all)
            part_there = jnp.exp(top_there - top_all)
            total = (
                part * stat_out[step, far, 1:2, :] + part_there * stat_in[step, 1 - far, 1:2, :]
            )
            inverse = 1.0 / total
            delta = (
                part * stat_out[step, far, 2:3, :] + part_there * stat_in[step, 1 - far, 2:3, :]
            ) * inverse
            factor = part * inverse
            query_sum = jnp.zeros((DH, 2 * TILE), jnp.float32)
            for pair in range(CHIPS):
                probs = expo[buffer, far, key_rows(pair), :] * factor
                score_grad = (
                    probs * (prob_grad[buffer, far, key_rows(pair), :] - delta) * score_scale
                ).astype(jnp.bfloat16)
                dv_sum[key_rows(pair), :] += jnp.dot(
                    probs.astype(jnp.bfloat16), grad_pair, preferred_element_type=jnp.float32
                )
                dk_sum[key_rows(pair), :] += jnp.dot(
                    score_grad, query_pair, preferred_element_type=jnp.float32
                )
                query_sum = query_sum + jnp.dot(
                    key_t[slot, pair], score_grad, preferred_element_type=jnp.float32
                )
            if far:
                part_out[step] = query_sum.T.astype(jnp.bfloat16)
                remote(
                    part_out.at[step],
                    part_in.at[step],
                    part_send.at[step],
                    part_recv.at[step],
                    mirror,
                ).start()
            else:
                dq_keep[buffer] = query_sum.T

        @pl.when(reach == CHIPS - 1)
        def _():
            dkv_out[slot, 0] = dk_sum[...].astype(jnp.bfloat16).reshape(SIDE_TILES, TILE, DH)
            dkv_out[slot, 1] = dv_sum[...].astype(jnp.bfloat16).reshape(SIDE_TILES, TILE, DH)
            head = head_of(slot)
            for place in reversed(range(SIDE_TILES)):
                give(
                    dkv_out.at[slot, :, place],
                    grads.at[pl.ds(1, 2), :, columns(head)],
                    1,
                    slot,
                    place // 2,
                    place % 2,
                    head,
                )

    def give(src, dst, which, slot, reach, turn, head):
        recv = out_recv.at[which, head]
        row_there, x_there = chip_at(reach)
        away = remote(
            src,
            dst,
            out_send.at[which, slot, 2 * reach + turn],
            recv,
            (seq_of(row_there, x_there, side), turn),
        )
        own = jnp.logical_and(reach == 0, core == turn)

        @pl.when(own)
        def _():
            pltpu.make_async_copy(src, dst, recv).start()

        @pl.when(jnp.logical_not(own))
        def _():
            away.start()

    def finish(step):
        slot = step // CHIPS
        reach = step % CHIPS
        settled(part_in.at[step], part_recv.at[step])
        total = dq_keep[step % 2] + part_in[step].astype(jnp.float32)
        dq_out[step] = total.astype(jnp.bfloat16).reshape(2, TILE, DH)
        head = head_of(slot)
        for turn in range(2):
            give(dq_out.at[step, turn], grads.at[0, :, columns(head)], 0, slot, reach, turn, head)

    def advance(step, _):
        @pl.when(step + RELAY_AHEAD < steps)
        def _():
            relay(step + RELAY_AHEAD)

        @pl.when(step < steps)
        def _():
            front(step)

        @pl.when(jnp.logical_and(step >= 1, step <= steps))
        def _():
            back(step - 1)

        @pl.when(step >= 2)
        def _():
            finish(step - 2)

        return 0

    lax.fori_loop(0, steps + 2, advance, 0)

    for index, send in enumerate(sends):
        src = send_parts(*send)[0]
        if send[3] or send[4]:
            settled(src, in_send.at[index])
        else:

            @pl.when(row != send[0])
            def _():
                settled(src, in_send.at[index])

    settled(lists_all.at[core], list_send.at[0])

    def drain(step, _):
        slot = step // CHIPS
        reach = step % CHIPS
        settled(stat_out.at[step], stat_send.at[step])
        settled(part_out.at[step], part_send.at[step])
        for turn in range(2):
            place = 2 * reach + turn
            settled(qg.at[slot, :, place], relay_send.at[slot, place])

            @pl.when(jnp.logical_not(jnp.logical_and(reach == 0, core == turn)))
            def _():
                settled(dq_out.at[step, turn], out_send.at[0, slot, place])
                settled(dkv_out.at[slot, :, place], out_send.at[1, slot, place])

        return 0

    lax.fori_loop(0, steps, drain, 0)

    def receive(head, _):
        settled(grads.at[0, :, columns(head)], out_recv.at[0, head])
        settled(grads.at[pl.ds(1, 2), :, columns(head)], out_recv.at[1, head])
        return 0

    lax.fori_loop(0, HEADS, receive, 0)


def settle_kernel(grads, *refs):
    copies = [pltpu.make_async_copy(grads.at[i], refs[i], refs[3].at[i]) for i in range(3)]
    for copy in copies:
        copy.start()
    for copy in copies:
        copy.wait()


def settle(grads):
    anywhere = pl.BlockSpec(memory_space=pl.ANY)
    return pl.pallas_call(
        settle_kernel,
        out_shape=[pltpu.HBM(grads.shape[1:], grads.dtype)] * 3,
        in_specs=[anywhere],
        out_specs=[anywhere] * 3,
        scratch_shapes=[pltpu.SemaphoreType.DMA((3,))],
    )(pltpu.with_memory_space_constraint(grads, pltpu.VMEM))


def half_body(queries, keys, values, out_grad, tile_lists):
    shape = (TILE, HEADS * DH)
    blocks = [array.reshape(shape) for array in (queries, keys, values, out_grad)]
    anywhere = pl.BlockSpec(memory_space=pl.ANY)
    side_rows = SIDE_TILES * TILE
    low = jnp.bfloat16
    full = jnp.float32
    dma = pltpu.SemaphoreType.DMA
    grads = pl.pallas_call(
        half_kernel,
        out_shape=pltpu.VMEM((3,) + shape, low),
        in_specs=[anywhere] * 5,
        out_specs=anywhere,
        scratch_shapes=[
            pltpu.VMEM((4,) + shape, low),
            pltpu.VMEM((INNER_SLOTS, 2, 2 * SIDE_TILES, TILE, DH), low),
            pltpu.VMEM((INNER_SLOTS, 2, SIDE_TILES, TILE, DH), low),
            pltpu.VMEM((TENSOR_DEVICES,) + tile_lists.shape, jnp.int32),
            pltpu.VMEM((2 * CHIPS, SIDE_TILES, 2 * TILE), full),
            pltpu.VMEM((INNER_SLOTS, CHIPS, DH, 2 * TILE), low),
            pltpu.VMEM((2, 2, side_rows, 2 * TILE), full),
            pltpu.VMEM((2, 2, side_rows, 2 * TILE), full),
            pltpu.VMEM((MAX_STEPS, 2, 8, 2 * TILE), full),
            pltpu.VMEM((MAX_STEPS, 2, 8, 2 * TILE), full),
            pltpu.VMEM((side_rows, DH), full),
            pltpu.VMEM((side_rows, DH), full),
            pltpu.VMEM((2, 2 * TILE, DH), full),
            pltpu.VMEM((MAX_STEPS, 2 * TILE, DH), low),
            pltpu.VMEM((MAX_STEPS, 2 * TILE, DH), low),
            pltpu.VMEM((MAX_STEPS, 2, TILE, DH), low),
            pltpu.VMEM((INNER_SLOTS, 2, SIDE_TILES, TILE, DH), low),
            dma((32,)),
            dma((2, INNER_SLOTS, SIDE_TILES)),
            dma((INNER_SLOTS, SIDE_TILES)),
            dma((INNER_SLOTS, SIDE_TILES)),
            dma((MAX_STEPS,)),
            dma((MAX_STEPS,)),
            dma((MAX_STEPS,)),
            dma((MAX_STEPS,)),
            dma((2, INNER_SLOTS, SIDE_TILES)),
            dma((2, HEADS)),
            dma((1,)),
            dma((TENSOR_DEVICES,)),
            dma((5,)),
        ],
        compiler_params=pltpu.CompilerParams(
            collective_id=0, has_side_effects=True, vmem_limit_bytes=60 * 1024 * 1024
        ),
    )(*blocks, tile_lists)
    return tuple(grad.reshape(queries.shape) for grad in settle(grads))


def body(queries, keys, values, out_grad, tile_lists):
    grid = (lax.axis_size("seq"), lax.axis_size("tensor"))
    if grid == (SEQ_DEVICES, TENSOR_DEVICES) and queries.shape == (1, TILE, HEADS * DH):
        return half_body(queries, keys, values, out_grad, tile_lists)
    return regrouped_body(queries, keys, values, out_grad, tile_lists)


def solution(mesh):
    return jax.shard_map(
        body,
        mesh=mesh,
        in_specs=(
            P(("groups", "tensor"), "seq", None),
            P(("groups", "tensor"), "seq", None),
            P(("groups", "tensor"), "seq", None),
            P(("groups", "tensor"), "seq", None),
            P(("groups", "tensor"), None),
        ),
        out_specs=(
            P(("groups", "tensor"), "seq", None),
            P(("groups", "tensor"), "seq", None),
            P(("groups", "tensor"), "seq", None),
        ),
        check_vma=False,
    )
```

```python
import functools
import math

import jax
import jax.numpy as jnp
from jax import lax
from jax.experimental import pallas as pl
from jax.experimental.pallas import tpu as pltpu
from jax.sharding import PartitionSpec as P

HEADS = 16
DH = 128
TILE = 128
RADIUS = 8
WIN = 12


block_tiles = 4


def padded_2(block, sides, width):
    for axis, dim in sides:
        count = lax.axis_size(axis)
        forward = [(i, i + 1) for i in range(count - 1)]
        backward = [(target, source) for source, target in forward]
        low = lax.ppermute(
            lax.slice_in_dim(block, block.shape[dim] - width, None, axis=dim), axis, forward
        )
        high = lax.ppermute(lax.slice_in_dim(block, 0, width, axis=dim), axis, backward)
        block = jnp.concatenate([low, block, high], axis=dim)
    return block


def key_rims(key_rows, value_rows):
    joined = jnp.concatenate([key_rows, value_rows], 1)
    return padded_2(joined, (("tensor", 0),), RADIUS * TILE)


def finish_rims(grads_ext, segment, local_width):
    rim_rows = RADIUS * TILE
    outer_rows = jnp.concatenate([grads_ext[:rim_rows], grads_ext[-rim_rows:]], 0)
    arrived = padded_2(outer_rows, (("tensor", 0),), rim_rows)
    own_rows = grads_ext[rim_rows : rim_rows + segment]
    own_rows = own_rows.at[:rim_rows].add(arrived[:rim_rows])
    own_rows = own_rows.at[segment - rim_rows :].add(arrived[3 * rim_rows :])
    own_rows = own_rows.astype(jnp.bfloat16)
    return (own_rows[:, :local_width], own_rows[:, local_width:])


def regrouped_body(queries, keys, values, out_grad, tile_lists):
    span_rows = queries.shape[1]
    feature_count = queries.shape[2]
    seq_count = lax.axis_size("seq")
    heads_here = HEADS // seq_count
    local_width = heads_here * DH
    score_scale = 1.0 / math.sqrt(DH)
    query_tokens = queries.reshape(span_rows, feature_count)
    key_tokens = keys.reshape(span_rows, feature_count)
    value_tokens = values.reshape(span_rows, feature_count)
    grad_tokens = out_grad.reshape(span_rows, feature_count)
    query_rows, key_rows, value_rows, grad_rows = (
        lax.all_to_all(query_tokens, "seq", split_axis=1, concat_axis=0, tiled=True),
        lax.all_to_all(key_tokens, "seq", split_axis=1, concat_axis=0, tiled=True),
        lax.all_to_all(value_tokens, "seq", split_axis=1, concat_axis=0, tiled=True),
        lax.all_to_all(grad_tokens, "seq", split_axis=1, concat_axis=0, tiled=True),
    )
    padded = key_rims(key_rows, value_rows)
    segment = query_rows.shape[0]
    seg_tiles = segment // TILE
    ext_tiles = seg_tiles + 2 * RADIUS
    block_count = seg_tiles // block_tiles
    first_tile = lax.axis_index("tensor") * seg_tiles - RADIUS
    kv_tiles = padded.reshape(ext_tiles, TILE, 2 * local_width)
    query_blocks = query_rows.reshape(block_count, block_tiles, TILE, heads_here, DH)
    grad_blocks = grad_rows.reshape(block_count, block_tiles, TILE, heads_here, DH)
    list_blocks = tile_lists.reshape(block_count, block_tiles, WIN)

    def attend_block(totals, inputs):
        query_block, grad_block, tile_rows = inputs
        present = tile_rows >= 0
        local_tile = jnp.clip(tile_rows - first_tile, 0, ext_tiles - 1)
        picked = jnp.concatenate(
            [
                lax.dynamic_slice_in_dim(kv_tiles, local_tile[row, entry], 1, 0)
                for row in range(block_tiles)
                for entry in range(WIN)
            ],
            0,
        ).reshape(block_tiles, WIN * TILE, 2, heads_here, DH)
        key_sel = picked[:, :, 0]
        value_sel = picked[:, :, 1]
        scores = (
            jnp.einsum("gthd,gkhd->ghtk", query_block, key_sel, preferred_element_type=jnp.float32)
            * score_scale
        )
        live_keys = jnp.repeat(present, TILE, axis=1)
        scores = jnp.where(live_keys[:, None, None, :], scores, -1e30)
        row_max = jnp.max(scores, axis=3, keepdims=True)
        weights = jnp.exp(scores - row_max)
        weights = weights / jnp.sum(weights, axis=3, keepdims=True)
        weights_b = weights.astype(jnp.bfloat16)
        recomputed = jnp.einsum(
            "ghtk,gkhd->gthd", weights_b, value_sel, preferred_element_type=jnp.float32
        )
        delta = jnp.sum(grad_block.astype(jnp.float32) * recomputed, axis=3)
        prob_grad = jnp.einsum(
            "gthd,gkhd->ghtk", grad_block, value_sel, preferred_element_type=jnp.float32
        )
        score_grad = (
            weights * (prob_grad - jnp.transpose(delta, (0, 2, 1))[..., None]) * score_scale
        ).astype(jnp.bfloat16)
        query_part = jnp.einsum(
            "ghtk,gkhd->gthd", score_grad, key_sel, preferred_element_type=jnp.float32
        ).astype(jnp.bfloat16)
        key_part = jnp.einsum(
            "ghtk,gthd->gkhd", score_grad, query_block, preferred_element_type=jnp.float32
        )
        value_part = jnp.einsum(
            "ghtk,gthd->gkhd", weights_b, grad_block, preferred_element_type=jnp.float32
        )
        key_terms = jnp.concatenate([key_part, value_part], 2).reshape(
            block_tiles, WIN, TILE, 2 * local_width
        )
        totals = totals.at[local_tile].add(key_terms)
        return (totals, query_part)

    initial = jnp.zeros((ext_tiles, TILE, 2 * local_width), jnp.float32)
    grads_ext, query_parts = lax.scan(
        attend_block, initial, (query_blocks, grad_blocks, list_blocks)
    )
    query_grad = query_parts.reshape(segment, local_width)
    grads_ext = grads_ext.reshape(ext_tiles * TILE, 2 * local_width)
    query_back = lax.all_to_all(query_grad, "seq", split_axis=0, concat_axis=1, tiled=True)
    key_grad, value_grad = finish_rims(grads_ext, segment, local_width)
    key_back, value_back = (
        lax.all_to_all(key_grad, "seq", split_axis=0, concat_axis=1, tiled=True),
        lax.all_to_all(value_grad, "seq", split_axis=0, concat_axis=1, tiled=True),
    )
    out_shape = queries.shape
    return (
        query_back.reshape(out_shape),
        key_back.reshape(out_shape),
        value_back.reshape(out_shape),
    )


def partner_order(seq_count, tensor_count):
    order = []
    for step in range(seq_count):
        reach = (seq_count // 2 + ((step + 1) // 2) * (1 - 2 * (step % 2))) % seq_count
        for turn in range(tensor_count):
            if reach or turn:
                order.append((reach, turn))
    return order


def head_kernel(
    seq_count,
    tensor_count,
    q_hbm,
    k_hbm,
    v_hbm,
    g_hbm,
    lists_hbm,
    dq_hbm,
    dk_hbm,
    dv_hbm,
    qk_all,
    v_all,
    g_all,
    lists_all,
    bias,
    probs,
    prob_grad,
    key_t,
    dv_sum,
    dk_sum,
    dq_out,
    dk_out,
    dv_out,
    staged,
    in_send,
    in_recv,
    out_send,
    out_recv,
    list_send,
    list_recv,
    local_sem,
):
    seq_here = lax.axis_index("seq")
    tensor_here = lax.axis_index("tensor")
    me = tensor_here * seq_count + seq_here
    tiles = seq_count * tensor_count
    pairs = tiles // 2
    score_scale = 1.0 / math.sqrt(DH)
    partners = []
    for reach, turn in partner_order(seq_count, tensor_count):
        seq_there = lax.rem(seq_here + reach, seq_count)
        tensor_there = lax.rem(tensor_here + turn, tensor_count)
        partners.append((seq_there, tensor_there, tensor_there * seq_count + seq_there))

    def columns(index):
        return pl.ds(pl.multiple_of(index * DH, DH), DH)

    def remote(src, dst, send, recv, seq_there, tensor_there):
        return pltpu.make_async_remote_copy(
            src_ref=src,
            dst_ref=dst,
            send_sem=send,
            recv_sem=recv,
            device_id={"seq": seq_there, "tensor": tensor_there},
            device_id_type=pl.DeviceIdType.MESH,
        )

    staging = [
        pltpu.make_async_copy(src, staged.at[which], local_sem.at[8 + which])
        for which, src in enumerate((q_hbm, k_hbm, g_hbm, v_hbm))
    ]
    q_all, k_all = qk_all.at[0], qk_all.at[1]
    incoming = {
        0: (lambda cols: staged.at[pl.ds(0, 2), :, cols], lambda slot: qk_all.at[:, slot]),
        2: (lambda cols: staged.at[2, :, cols], lambda slot: g_all.at[slot]),
        3: (lambda cols: staged.at[3, :, cols], lambda slot: v_all.at[slot]),
    }
    outgoing = ((dv_out, dv_hbm), (dq_out, dq_hbm), (dk_out, dk_hbm))

    def in_copy(which, seq_there, tensor_there, there):
        src, dst = incoming[which]
        return remote(
            src(columns(there)),
            dst(me),
            in_send.at[which, there],
            in_recv.at[which, me],
            seq_there,
            tensor_there,
        )

    def in_wait(which, seq_there, tensor_there, there):
        src, dst = incoming[which]
        remote(
            src(columns(there)),
            dst(there),
            in_send.at[which, there],
            in_recv.at[which, there],
            seq_there,
            tensor_there,
        ).wait()

    def in_local(which):
        src, dst = incoming[which]
        return pltpu.make_async_copy(src(columns(me)), dst(me), local_sem.at[which])

    def out_copy(which, seq_there, tensor_there, there):
        src, dst = outgoing[which]
        return remote(
            src.at[there],
            dst.at[:, columns(me)],
            out_send.at[which, there],
            out_recv.at[which, me],
            seq_there,
            tensor_there,
        )

    def out_wait(which, seq_there, tensor_there, there):
        src, dst = outgoing[which]
        remote(
            src.at[there],
            dst.at[:, columns(there)],
            out_send.at[which, there],
            out_recv.at[which, there],
            seq_there,
            tensor_there,
        ).wait()

    def out_local(which):
        src, dst = outgoing[which]
        return pltpu.make_async_copy(src.at[me], dst.at[:, columns(me)], local_sem.at[4 + which])

    for copy in staging:
        copy.start()
    own_list = pltpu.make_async_copy(lists_hbm, lists_all.at[tensor_here], local_sem.at[7])
    own_list.start()

    barrier = pltpu.get_barrier_semaphore()
    for seq_there, tensor_there, _ in partners:
        pl.semaphore_signal(
            barrier,
            inc=1,
            device_id={"seq": seq_there, "tensor": tensor_there},
            device_id_type=pl.DeviceIdType.MESH,
        )
    pl.semaphore_wait(barrier, len(partners))

    def list_copy(turn, slot):
        return remote(
            lists_hbm,
            lists_all.at[slot],
            list_send.at[turn],
            list_recv.at[slot],
            seq_here,
            lax.rem(tensor_here + turn, tensor_count),
        )

    for turn in range(1, tensor_count):
        list_copy(turn, tensor_here).start()
    for group in ((0, 1), (2,), (3,)):
        for which in group:
            staging[which].wait()
        in_local(group[0]).start()
        for partner in partners:
            in_copy(group[0], *partner).start()

    own_list.wait()
    for turn in range(1, tensor_count):
        list_copy(turn, lax.rem(tensor_here + turn, tensor_count)).wait()
    tile_ids = lax.broadcasted_iota(jnp.int32, (tiles, TILE), 0)
    for tile in range(tiles):
        row = lists_all[tile // seq_count, tile % seq_count : tile % seq_count + 1, :]
        miss = jnp.full((tiles, TILE), -1e30, jnp.float32)
        for entry in range(WIN):
            miss = jnp.where(row[:, entry : entry + 1] == tile_ids, 0.0, miss)
        half = (tile % 2) * TILE
        bias[tile // 2, :, half : half + TILE] = miss

    dv_sum[...] = jnp.zeros_like(dv_sum)
    dk_sum[...] = jnp.zeros_like(dk_sum)

    in_local(0).wait()
    for partner in partners:
        in_wait(0, *partner)

    def pair_rows(ref, index):
        return ref[pl.ds(2 * index, 2)].reshape(2 * TILE, DH)

    def turned(block):
        return block.astype(jnp.float32).T.astype(jnp.bfloat16)

    def key_rows(index):
        return pl.ds(index * 2 * TILE, 2 * TILE)

    def fold(block, op):
        return op(block.reshape(2 * TILE // 8, 8, 2 * TILE), axis=0)

    def score_pair(pair, _):
        query_t = turned(pair_rows(q_all, pair))
        key_t[pair] = turned(pair_rows(k_all, pair))
        top = jnp.full((8, 2 * TILE), -3e38, jnp.float32)
        for chunk in range(pairs):
            scores = (
                jnp.dot(pair_rows(k_all, chunk), query_t, preferred_element_type=jnp.float32)
                * score_scale
            )
            scores = jnp.concatenate(
                [
                    scores[:TILE] + bias[pair, 2 * chunk : 2 * chunk + 1, :],
                    scores[TILE:] + bias[pair, 2 * chunk + 1 : 2 * chunk + 2, :],
                ],
                axis=0,
            )
            probs[pair, key_rows(chunk), :] = scores
            top = jnp.maximum(top, fold(scores, jnp.max))
        top = jnp.max(top, axis=0, keepdims=True)
        total = jnp.zeros((8, 2 * TILE), jnp.float32)
        for chunk in range(pairs):
            weights = jnp.exp(probs[pair, key_rows(chunk), :] - top)
            probs[pair, key_rows(chunk), :] = weights
            total = total + fold(weights, jnp.sum)
        inverse = 1.0 / jnp.sum(total, axis=0, keepdims=True)
        for chunk in range(pairs):
            probs[pair, key_rows(chunk), :] = probs[pair, key_rows(chunk), :] * inverse
        return 0

    lax.fori_loop(0, pairs, score_pair, 0)

    in_local(2).wait()
    for partner in partners:
        in_wait(2, *partner)

    def value_pair(pair, _):
        grad_pair = pair_rows(g_all, pair)
        for chunk in range(pairs):
            dv_sum[key_rows(chunk), :] += jnp.dot(
                probs[pair, key_rows(chunk), :].astype(jnp.bfloat16),
                grad_pair,
                preferred_element_type=jnp.float32,
            )
        return 0

    lax.fori_loop(0, pairs, value_pair, 0)
    dv_out[...] = dv_sum[...].astype(jnp.bfloat16).reshape(dv_out.shape)
    for partner in partners:
        out_copy(0, *partner).start()
    out_local(0).start()

    in_local(3).wait()
    for partner in partners:
        in_wait(3, *partner)

    def grad_pair_step(pair, _):
        query_pair = pair_rows(q_all, pair)
        grad_t = turned(pair_rows(g_all, pair))
        delta = jnp.zeros((8, 2 * TILE), jnp.float32)
        for chunk in range(pairs):
            product = jnp.dot(pair_rows(v_all, chunk), grad_t, preferred_element_type=jnp.float32)
            prob_grad[key_rows(chunk), :] = product
            rounded = probs[pair, key_rows(chunk), :].astype(jnp.bfloat16).astype(jnp.float32)
            delta = delta + fold(rounded * product, jnp.sum)
        delta = jnp.sum(delta, axis=0, keepdims=True)
        query_sum = jnp.zeros((DH, 2 * TILE), jnp.float32)
        for chunk in range(pairs):
            score_grad = (
                probs[pair, key_rows(chunk), :]
                * (prob_grad[key_rows(chunk), :] - delta)
                * score_scale
            ).astype(jnp.bfloat16)
            dk_sum[key_rows(chunk), :] += jnp.dot(
                score_grad, query_pair, preferred_element_type=jnp.float32
            )
            query_sum = query_sum + jnp.dot(
                key_t[chunk], score_grad, preferred_element_type=jnp.float32
            )
        dq_out[pl.ds(2 * pair, 2)] = query_sum.T.astype(jnp.bfloat16).reshape(2, TILE, DH)
        for side in range(2):
            there = 2 * pair + side

            @pl.when(there != me)
            def _():
                out_copy(1, lax.rem(there, seq_count), there // seq_count, there).start()

        return 0

    lax.fori_loop(0, pairs, grad_pair_step, 0)
    dk_out[...] = dk_sum[...].astype(jnp.bfloat16).reshape(dk_out.shape)
    for partner in partners:
        out_copy(2, *partner).start()
    out_local(1).start()
    out_local(2).start()

    for which in range(3):
        out_local(which).wait()
        for partner in partners:
            out_wait(which, *partner)


def settle_kernel(*refs):
    copies = [
        pltpu.make_async_copy(src, dst, refs[6].at[i])
        for i, (src, dst) in enumerate(zip(refs[:3], refs[3:6]))
    ]
    for copy in copies:
        copy.start()
    for copy in copies:
        copy.wait()


def settle(grads):
    anywhere = pl.BlockSpec(memory_space=pl.ANY)
    return pl.pallas_call(
        settle_kernel,
        out_shape=[pltpu.HBM(grad.shape, grad.dtype) for grad in grads],
        in_specs=[anywhere] * 3,
        out_specs=[anywhere] * 3,
        scratch_shapes=[pltpu.SemaphoreType.DMA((3,))],
    )(*[pltpu.with_memory_space_constraint(grad, pltpu.VMEM) for grad in grads])


def head_body(queries, keys, values, out_grad, tile_lists):
    seq_count = lax.axis_size("seq")
    tensor_count = lax.axis_size("tensor")
    tiles = seq_count * tensor_count
    pairs = tiles // 2
    shape = (TILE, HEADS * DH)
    blocks = [array.reshape(shape) for array in (queries, keys, values, out_grad)]
    anywhere = pl.BlockSpec(memory_space=pl.ANY)
    per_tile = pltpu.VMEM((tiles, TILE, DH), jnp.bfloat16)
    grads = pl.pallas_call(
        functools.partial(head_kernel, seq_count, tensor_count),
        out_shape=[pltpu.VMEM(shape, jnp.bfloat16)] * 3,
        in_specs=[anywhere] * 5,
        out_specs=[anywhere] * 3,
        scratch_shapes=[
            pltpu.VMEM((2, tiles, TILE, DH), jnp.bfloat16),
            per_tile,
            per_tile,
            pltpu.VMEM((tensor_count,) + tile_lists.shape, jnp.int32),
            pltpu.VMEM((pairs, tiles, 2 * TILE), jnp.float32),
            pltpu.VMEM((pairs, tiles * TILE, 2 * TILE), jnp.float32),
            pltpu.VMEM((tiles * TILE, 2 * TILE), jnp.float32),
            pltpu.VMEM((pairs, DH, 2 * TILE), jnp.bfloat16),
            pltpu.VMEM((tiles * TILE, DH), jnp.float32),
            pltpu.VMEM((tiles * TILE, DH), jnp.float32),
            per_tile,
            per_tile,
            per_tile,
            pltpu.VMEM((4,) + shape, jnp.bfloat16),
            pltpu.SemaphoreType.DMA((4, tiles)),
            pltpu.SemaphoreType.DMA((4, tiles)),
            pltpu.SemaphoreType.DMA((3, tiles)),
            pltpu.SemaphoreType.DMA((3, tiles)),
            pltpu.SemaphoreType.DMA((tensor_count,)),
            pltpu.SemaphoreType.DMA((tensor_count,)),
            pltpu.SemaphoreType.DMA((12,)),
        ],
        compiler_params=pltpu.CompilerParams(
            collective_id=0, has_side_effects=True, vmem_limit_bytes=60 * 1024 * 1024
        ),
    )(*blocks, tile_lists)
    return tuple(grad.reshape(queries.shape) for grad in settle(grads))


def body(queries, keys, values, out_grad, tile_lists):
    devices = lax.axis_size("seq") * lax.axis_size("tensor")
    one_head_one_tile = devices == HEADS and queries.shape[:2] == (1, TILE)
    if one_head_one_tile and queries.shape[2] == HEADS * DH:
        return head_body(queries, keys, values, out_grad, tile_lists)
    return regrouped_body(queries, keys, values, out_grad, tile_lists)


def solution(mesh):
    return jax.shard_map(
        body,
        mesh=mesh,
        in_specs=(
            P(("groups", "tensor"), "seq", None),
            P(("groups", "tensor"), "seq", None),
            P(("groups", "tensor"), "seq", None),
            P(("groups", "tensor"), "seq", None),
            P(("groups", "tensor"), None),
        ),
        out_specs=(
            P(("groups", "tensor"), "seq", None),
            P(("groups", "tensor"), "seq", None),
            P(("groups", "tensor"), "seq", None),
        ),
        check_vma=False,
    )
```

```python
import functools
import math

import jax
import jax.numpy as jnp
from jax import lax
from jax.experimental import pallas as pl
from jax.experimental.pallas import tpu as pltpu
from jax.sharding import PartitionSpec as P

HEADS = 16
DH = 128
TILE = 128
RADIUS = 8
WIN = 12


block_tiles = 4


def padded_2(block, sides, width):
    for axis, dim in sides:
        count = lax.axis_size(axis)
        forward = [(i, i + 1) for i in range(count - 1)]
        backward = [(target, source) for source, target in forward]
        low = lax.ppermute(
            lax.slice_in_dim(block, block.shape[dim] - width, None, axis=dim), axis, forward
        )
        high = lax.ppermute(lax.slice_in_dim(block, 0, width, axis=dim), axis, backward)
        block = jnp.concatenate([low, block, high], axis=dim)
    return block


def key_rims(key_rows, value_rows):
    joined = jnp.concatenate([key_rows, value_rows], 1)
    return padded_2(joined, (("tensor", 0),), RADIUS * TILE)


def finish_rims(grads_ext, segment, local_width):
    rim_rows = RADIUS * TILE
    outer_rows = jnp.concatenate([grads_ext[:rim_rows], grads_ext[-rim_rows:]], 0)
    arrived = padded_2(outer_rows, (("tensor", 0),), rim_rows)
    own_rows = grads_ext[rim_rows : rim_rows + segment]
    own_rows = own_rows.at[:rim_rows].add(arrived[:rim_rows])
    own_rows = own_rows.at[segment - rim_rows :].add(arrived[3 * rim_rows :])
    own_rows = own_rows.astype(jnp.bfloat16)
    return (own_rows[:, :local_width], own_rows[:, local_width:])


def regrouped_body(queries, keys, values, out_grad, tile_lists):
    span_rows = queries.shape[1]
    feature_count = queries.shape[2]
    seq_count = lax.axis_size("seq")
    heads_here = HEADS // seq_count
    local_width = heads_here * DH
    score_scale = 1.0 / math.sqrt(DH)
    query_tokens = queries.reshape(span_rows, feature_count)
    key_tokens = keys.reshape(span_rows, feature_count)
    value_tokens = values.reshape(span_rows, feature_count)
    grad_tokens = out_grad.reshape(span_rows, feature_count)
    query_rows, key_rows, value_rows, grad_rows = (
        lax.all_to_all(query_tokens, "seq", split_axis=1, concat_axis=0, tiled=True),
        lax.all_to_all(key_tokens, "seq", split_axis=1, concat_axis=0, tiled=True),
        lax.all_to_all(value_tokens, "seq", split_axis=1, concat_axis=0, tiled=True),
        lax.all_to_all(grad_tokens, "seq", split_axis=1, concat_axis=0, tiled=True),
    )
    padded = key_rims(key_rows, value_rows)
    segment = query_rows.shape[0]
    seg_tiles = segment // TILE
    ext_tiles = seg_tiles + 2 * RADIUS
    block_count = seg_tiles // block_tiles
    first_tile = lax.axis_index("tensor") * seg_tiles - RADIUS
    kv_tiles = padded.reshape(ext_tiles, TILE, 2 * local_width)
    query_blocks = query_rows.reshape(block_count, block_tiles, TILE, heads_here, DH)
    grad_blocks = grad_rows.reshape(block_count, block_tiles, TILE, heads_here, DH)
    list_blocks = tile_lists.reshape(block_count, block_tiles, WIN)

    def attend_block(totals, inputs):
        query_block, grad_block, tile_rows = inputs
        present = tile_rows >= 0
        local_tile = jnp.clip(tile_rows - first_tile, 0, ext_tiles - 1)
        picked = jnp.concatenate(
            [
                lax.dynamic_slice_in_dim(kv_tiles, local_tile[row, entry], 1, 0)
                for row in range(block_tiles)
                for entry in range(WIN)
            ],
            0,
        ).reshape(block_tiles, WIN * TILE, 2, heads_here, DH)
        key_sel = picked[:, :, 0]
        value_sel = picked[:, :, 1]
        scores = (
            jnp.einsum("gthd,gkhd->ghtk", query_block, key_sel, preferred_element_type=jnp.float32)
            * score_scale
        )
        live_keys = jnp.repeat(present, TILE, axis=1)
        scores = jnp.where(live_keys[:, None, None, :], scores, -1e30)
        row_max = jnp.max(scores, axis=3, keepdims=True)
        weights = jnp.exp(scores - row_max)
        weights = weights / jnp.sum(weights, axis=3, keepdims=True)
        weights_b = weights.astype(jnp.bfloat16)
        recomputed = jnp.einsum(
            "ghtk,gkhd->gthd", weights_b, value_sel, preferred_element_type=jnp.float32
        )
        delta = jnp.sum(grad_block.astype(jnp.float32) * recomputed, axis=3)
        prob_grad = jnp.einsum(
            "gthd,gkhd->ghtk", grad_block, value_sel, preferred_element_type=jnp.float32
        )
        score_grad = (
            weights * (prob_grad - jnp.transpose(delta, (0, 2, 1))[..., None]) * score_scale
        ).astype(jnp.bfloat16)
        query_part = jnp.einsum(
            "ghtk,gkhd->gthd", score_grad, key_sel, preferred_element_type=jnp.float32
        ).astype(jnp.bfloat16)
        key_part = jnp.einsum(
            "ghtk,gthd->gkhd", score_grad, query_block, preferred_element_type=jnp.float32
        )
        value_part = jnp.einsum(
            "ghtk,gthd->gkhd", weights_b, grad_block, preferred_element_type=jnp.float32
        )
        key_terms = jnp.concatenate([key_part, value_part], 2).reshape(
            block_tiles, WIN, TILE, 2 * local_width
        )
        totals = totals.at[local_tile].add(key_terms)
        return (totals, query_part)

    initial = jnp.zeros((ext_tiles, TILE, 2 * local_width), jnp.float32)
    grads_ext, query_parts = lax.scan(
        attend_block, initial, (query_blocks, grad_blocks, list_blocks)
    )
    query_grad = query_parts.reshape(segment, local_width)
    grads_ext = grads_ext.reshape(ext_tiles * TILE, 2 * local_width)
    query_back = lax.all_to_all(query_grad, "seq", split_axis=0, concat_axis=1, tiled=True)
    key_grad, value_grad = finish_rims(grads_ext, segment, local_width)
    key_back, value_back = (
        lax.all_to_all(key_grad, "seq", split_axis=0, concat_axis=1, tiled=True),
        lax.all_to_all(value_grad, "seq", split_axis=0, concat_axis=1, tiled=True),
    )
    out_shape = queries.shape
    return (
        query_back.reshape(out_shape),
        key_back.reshape(out_shape),
        value_back.reshape(out_shape),
    )


SEQ_DEVICES = 8
TENSOR_DEVICES = 2
SIDE_TILES = 8
CHIPS = 4
INNER_SLOTS = 3
MAX_STEPS = INNER_SLOTS * CHIPS
WIDE = 4 * TILE
LOG2_E = 1.0 / math.log(2.0)
SEND_ORDER = (
    (1, 0, 0, 0),
    (1, 0, 1, 0),
    (0, 0, 0, 1),
    (0, 0, 0, 0),
    (0, 0, 1, 0),
    (1, 1, 0, 0),
    (1, 2, 0, 0),
    (1, 1, 1, 0),
    (1, 2, 1, 0),
)
RELAY_FIRST = ((0, 0), (0, 1), (0, 2), (0, 3), (1, 0), (1, 1), (2, 0), (2, 1))
RELAY_AT = {
    2: ((1, 2),),
    3: ((1, 3),),
    4: ((2, 2),),
    5: ((2, 3),),
}
BACK_LAG = (3, 5)
PART_LAG = (1, 2)
FINISH_LAG = (6, 9)
BUFFERS = max(BACK_LAG) + 1
KEPT = max(FINISH_LAG) + 1


def half_kernel(
    q_hbm,
    k_hbm,
    v_hbm,
    g_hbm,
    lists_hbm,
    grads,
    staged,
    qg,
    kv,
    lists_all,
    bias,
    key_t,
    expo,
    prob_grad,
    stat_out,
    stat_in,
    inverse_sum,
    dv_sum,
    dk_sum,
    dq_keep,
    part_out,
    part_in,
    dq_out,
    dkv_out,
    in_send,
    in_recv,
    relay_send,
    relay_recv,
    stat_send,
    stat_recv,
    part_send,
    part_recv,
    out_send,
    out_recv,
    list_send,
    list_recv,
    local_sem,
):
    seq_here = lax.axis_index("seq")
    core = lax.axis_index("tensor")
    z_here = seq_here // 2
    x_here = lax.rem(seq_here, 2)
    side = z_here // 2
    row = z_here + side * (3 - 2 * z_here)
    steps = CHIPS * (1 + 2 * row)
    score_scale = 1.0 / math.sqrt(DH)
    back_lag, part_lag, finish_lag = (
        lags[0] + row * (lags[1] - lags[0]) for lags in (BACK_LAG, PART_LAG, FINISH_LAG)
    )

    def seq_of(row_there, x_there, side_there):
        return 2 * (row_there + side_there * (3 - 2 * row_there)) + x_there

    def chip_at(reach):
        row_there = lax.rem(row + reach // 2, 2)
        x_there = lax.rem(x_here + reach % 2, 2)
        return row_there, x_there

    def head_of(slot):
        return row * 4 * slot + (1 - row) * 4 * INNER_SLOTS + 2 * x_here + core

    mirror = (seq_of(row, x_here, 1 - side), core)

    def columns(index):
        return pl.ds(pl.multiple_of(index * DH, DH), DH)

    def remote(src, dst, send, recv, there):
        return pltpu.make_async_remote_copy(
            src_ref=src,
            dst_ref=dst,
            send_sem=send,
            recv_sem=recv,
            device_id={"seq": there[0], "tensor": there[1]},
            device_id_type=pl.DeviceIdType.MESH,
        )

    def settled(ref, sem):
        pltpu.make_async_copy(ref, ref, sem).wait()

    staging = [
        pltpu.make_async_copy(src, staged.at[which], local_sem.at[which])
        for which, src in enumerate((q_hbm, g_hbm, k_hbm, v_hbm))
    ]
    for copy in staging:
        copy.start()
    own_list = pltpu.make_async_copy(lists_hbm, lists_all.at[core], local_sem.at[4])
    own_list.start()

    barrier = pltpu.get_barrier_semaphore()
    greeted = []
    for turn in range(2):
        for far in range(2):
            for reach in range(CHIPS):
                if turn or far or reach:
                    row_there, x_there = chip_at(reach)
                    side_there = lax.rem(side + far, 2)
                    greeted.append((seq_of(row_there, x_there, side_there), lax.rem(core + turn, 2)))
    for there in greeted:
        pl.semaphore_signal(
            barrier,
            inc=1,
            device_id={"seq": there[0], "tensor": there[1]},
            device_id_type=pl.DeviceIdType.MESH,
        )
    pl.semaphore_wait(barrier, len(greeted))

    other_core = lax.rem(core + 1, 2)
    remote(
        lists_hbm, lists_all.at[core], list_send.at[0], list_recv.at[core], (seq_here, other_core)
    ).start()

    sends = [
        (row_there, slot, which, far, dx, dc)
        for row_there, slot, which, far in SEND_ORDER
        for dx in range(2)
        for dc in range(2)
    ]

    def send_parts(row_there, slot, which, far, dx, dc):
        x_there = lax.rem(x_here + dx, 2)
        core_there = lax.rem(core + dc, 2)
        head = (4 * slot if row_there else 4 * INNER_SLOTS) + 2 * x_there + core_there
        reach = 2 * lax.rem(row + row_there, 2) + dx
        place = 2 * reach + core
        src = staged.at[pl.ds(2 * which, 2), :, columns(head)]
        dst = (kv if which else qg).at[slot, :, SIDE_TILES * far + place]
        recv = relay_recv.at[slot, place] if far else in_recv.at[which, slot, place]
        side_there = lax.rem(side + far, 2)
        return src, dst, recv, (seq_of(row_there, x_there, side_there), core_there)

    def stays_here(row_there, slot, which, far, dx, dc):
        return not (far or dx or dc)

    staged_yet = [False, False]
    for index, send in enumerate(sends):
        if not staged_yet[send[2]]:
            staged_yet[send[2]] = True
            for copy in staging[2 * send[2] : 2 * send[2] + 2]:
                copy.wait()
        src, dst, recv, there = send_parts(*send)
        away = remote(src, dst, in_send.at[index], recv, there)
        if stays_here(*send):
            stays = pltpu.make_async_copy(src, dst, recv)

            @pl.when(row == send[0])
            def _():
                stays.start()

            @pl.when(row != send[0])
            def _():
                away.start()
        else:
            away.start()

    def relay(slot, reach):
        for turn in range(2):
            place = 2 * reach + turn
            block = qg.at[slot, :, place]
            settled(block, in_recv.at[0, slot, place])
            remote(
                block,
                qg.at[slot, :, SIDE_TILES + place],
                relay_send.at[slot, place],
                relay_recv.at[slot, place],
                mirror,
            ).start()

    @pl.when(row == 1)
    def _():
        for slot, reach in RELAY_FIRST:
            relay(slot, reach)

    own_list.wait()
    settled(lists_all.at[other_core], list_recv.at[other_core])
    ids = lax.broadcasted_iota(jnp.int32, (SIDE_TILES, TILE), 0)
    id_row = lax.rem(row + ids // 4, 2)
    id_x = lax.rem(x_here + lax.rem(ids // 2, 2), 2)
    key_ids = 8 * lax.rem(ids, 2) + 2 * (id_row + side * (3 - 2 * id_row)) + id_x
    for chunk in range(2 * CHIPS):
        row_there, x_there = chip_at(chunk % CHIPS)
        chip = seq_of(row_there, x_there, side if chunk < CHIPS else 1 - side)
        for turn in range(2):
            listed = lists_all[turn, pl.ds(chip, 1), :]
            miss = jnp.full((SIDE_TILES, TILE), -1e30, jnp.float32)
            for entry in range(WIN):
                miss = jnp.where(listed[:, entry : entry + 1] == key_ids, 0.0, miss)
            at = 2 * (chunk // CHIPS) + turn
            bias[chunk % CHIPS, :, at * TILE : (at + 1) * TILE] = miss

    def turned(block):
        return block.astype(jnp.float32).T.astype(jnp.bfloat16)

    def across(left, right):
        return lax.dot_general(
            left, right, (((1,), (1,)), ((), ())), preferred_element_type=jnp.float32
        )

    def pair_of(ref, slot, which, pair):
        return ref[slot, which, pl.ds(2 * pair, 2)].reshape(2 * TILE, DH)

    def key_rows(index):
        return slice(index * 2 * TILE, (index + 1) * 2 * TILE)

    def fold(block, op):
        return op(block.reshape(2 * TILE // 8, 8, WIDE), axis=0)

    def put_row(ref, step, index, line):
        for part in range(4):
            at = 4 * index + part
            ref[step, at : at + 1, :] = line[:, part * TILE : (part + 1) * TILE]

    def get_row(ref, step, index):
        return jnp.concatenate(
            [ref[step, 4 * index + part : 4 * index + part + 1, :] for part in range(4)], axis=1
        )

    def swapped(line):
        return jnp.concatenate([line[:, 2 * TILE :], line[:, : 2 * TILE]], axis=1)

    def front(step):
        slot = step // CHIPS
        reach = step % CHIPS
        buffer = step % BUFFERS

        @pl.when(reach == 0)
        def _():
            for place in range(SIDE_TILES):
                settled(kv.at[slot, :, place], in_recv.at[1, slot, place])
            for pair in range(CHIPS):
                key_t[slot, pair] = turned(pair_of(kv, slot, 0, pair))

        @pl.when(row == 0)
        def _():
            for turn in range(2):
                place = 2 * reach + turn
                settled(qg.at[slot, :, place], in_recv.at[0, slot, place])

        for turn in range(2):
            place = 2 * reach + turn
            settled(qg.at[slot, :, SIDE_TILES + place], relay_recv.at[slot, place])
        query_rows = jnp.concatenate(
            [pair_of(qg, slot, 0, CHIPS * far + reach) for far in range(2)], axis=0
        )
        grad_rows = jnp.concatenate(
            [pair_of(qg, slot, 1, CHIPS * far + reach) for far in range(2)], axis=0
        )
        top = jnp.full((8, WIDE), -3e38, jnp.float32)
        for pair in range(CHIPS):
            scores = across(pair_of(kv, slot, 0, pair), query_rows)
            scores = jnp.concatenate(
                [
                    scores[:TILE] + bias[reach, 2 * pair : 2 * pair + 1, :],
                    scores[TILE:] + bias[reach, 2 * pair + 1 : 2 * pair + 2, :],
                ],
                axis=0,
            )
            expo[buffer, key_rows(pair), :] = scores
            top = jnp.maximum(top, fold(scores, jnp.max))
        top = jnp.max(top, axis=0, keepdims=True)
        total = jnp.zeros((8, WIDE), jnp.float32)
        delta = jnp.zeros((8, WIDE), jnp.float32)
        for pair in range(CHIPS):
            product = across(pair_of(kv, slot, 1, pair), grad_rows)
            weights = jnp.exp2(
                (expo[buffer, key_rows(pair), :] - top) * (score_scale * LOG2_E)
            )
            expo[buffer, key_rows(pair), :] = weights
            prob_grad[buffer, key_rows(pair), :] = product
            total = total + fold(weights, jnp.sum)
            delta = delta + fold(weights * product, jnp.sum)
        total = jnp.sum(total, axis=0, keepdims=True)
        inverse = 1.0 / total
        inverse_sum[buffer] = inverse
        put_row(stat_out, step, 0, top * score_scale + jnp.log(total))
        put_row(stat_out, step, 1, jnp.sum(delta, axis=0, keepdims=True) * inverse)
        remote(
            stat_out.at[step], stat_in.at[step], stat_send.at[step], stat_recv.at[step], mirror
        ).start()

    def back(step):
        slot = step // CHIPS
        reach = step % CHIPS
        buffer = step % BUFFERS

        @pl.when(reach == 0)
        def _():
            dv_sum[...] = jnp.zeros_like(dv_sum)
            dk_sum[...] = jnp.zeros_like(dk_sum)

        settled(stat_in.at[step], stat_recv.at[step])
        def both(which):
            return jnp.concatenate(
                [pair_of(qg, slot, which, CHIPS * far + reach) for far in range(2)], axis=0
            )

        query_rows, grad_rows = both(0), both(1)
        level = get_row(stat_out, step, 0)
        level_there = swapped(get_row(stat_in, step, 0))
        top_level = jnp.maximum(level, level_there)
        share = jnp.exp(level - top_level)
        share_there = jnp.exp(level_there - top_level)
        inverse = 1.0 / (share + share_there)
        delta = (
            share * get_row(stat_out, step, 1) + share_there * swapped(get_row(stat_in, step, 1))
        ) * inverse
        factor = share * inverse * inverse_sum[buffer]
        query_sum = jnp.zeros((DH, WIDE), jnp.float32)
        for pair in range(CHIPS):
            probs = expo[buffer, key_rows(pair), :] * factor
            score_grad = (
                probs * (prob_grad[buffer, key_rows(pair), :] - delta) * score_scale
            ).astype(jnp.bfloat16)
            dv_sum[key_rows(pair), :] += jnp.dot(
                probs.astype(jnp.bfloat16), grad_rows, preferred_element_type=jnp.float32
            )
            dk_sum[key_rows(pair), :] += jnp.dot(
                score_grad, query_rows, preferred_element_type=jnp.float32
            )
            query_sum = query_sum + jnp.dot(
                key_t[slot, pair], score_grad, preferred_element_type=jnp.float32
            )
        dq_keep[step % KEPT] = query_sum[:, : 2 * TILE]
        part_out[step] = query_sum[:, 2 * TILE :].astype(jnp.bfloat16)

        @pl.when(reach == CHIPS - 1)
        def _():
            dkv_out[slot, 0] = dk_sum[...].astype(jnp.bfloat16).reshape(SIDE_TILES, TILE, DH)
            dkv_out[slot, 1] = dv_sum[...].astype(jnp.bfloat16).reshape(SIDE_TILES, TILE, DH)
            head = head_of(slot)
            for place in reversed(range(SIDE_TILES)):
                give(
                    dkv_out.at[slot, :, place],
                    grads.at[pl.ds(1, 2), :, columns(head)],
                    1,
                    slot,
                    place // 2,
                    place % 2,
                    head,
                )

    def pass_part(step):
        remote(
            part_out.at[step], part_in.at[step], part_send.at[step], part_recv.at[step], mirror
        ).start()

    def give(src, dst, which, slot, reach, turn, head):
        recv = out_recv.at[which, head]
        row_there, x_there = chip_at(reach)
        away = remote(
            src,
            dst,
            out_send.at[which, slot, 2 * reach + turn],
            recv,
            (seq_of(row_there, x_there, side), turn),
        )
        own = jnp.logical_and(reach == 0, core == turn)

        @pl.when(own)
        def _():
            pltpu.make_async_copy(src, dst, recv).start()

        @pl.when(jnp.logical_not(own))
        def _():
            away.start()

    def finish(step):
        slot = step // CHIPS
        reach = step % CHIPS
        settled(part_in.at[step], part_recv.at[step])
        total = dq_keep[step % KEPT] + part_in[step].astype(jnp.float32)
        dq_out[step] = total.T.astype(jnp.bfloat16).reshape(2, TILE, DH)
        head = head_of(slot)
        for turn in range(2):
            give(dq_out.at[step, turn], grads.at[0, :, columns(head)], 0, slot, reach, turn, head)

    def advance(step, _):
        for due, blocks in RELAY_AT.items():

            @pl.when(jnp.logical_and(row == 1, step == due))
            def _():
                for slot, reach in blocks:
                    relay(slot, reach)

        @pl.when(step < steps)
        def _():
            front(step)

        def delayed(stage, lag):
            @pl.when(jnp.logical_and(step >= lag, step < steps + lag))
            def _():
                stage(step - lag)

        delayed(back, back_lag)
        last_back = steps + back_lag - 1

        @pl.when(jnp.logical_and(step >= back_lag + part_lag, step < last_back))
        def _():
            pass_part(step - back_lag - part_lag)

        @pl.when(step == last_back)
        def _():
            def pass_rest(rest, _):
                pass_part(rest)
                return 0

            lax.fori_loop(jnp.maximum(steps - 1 - part_lag, 0), steps, pass_rest, 0)

        delayed(finish, back_lag + finish_lag)
        return 0

    lax.fori_loop(0, steps + back_lag + finish_lag, advance, 0)

    for index, send in enumerate(sends):
        src = send_parts(*send)[0]
        if stays_here(*send):

            @pl.when(row != send[0])
            def _():
                settled(src, in_send.at[index])
        else:
            settled(src, in_send.at[index])

    settled(lists_all.at[core], list_send.at[0])

    def drain(step, _):
        slot = step // CHIPS
        reach = step % CHIPS
        settled(stat_out.at[step], stat_send.at[step])
        settled(part_out.at[step], part_send.at[step])
        for turn in range(2):
            place = 2 * reach + turn

            @pl.when(row == 1)
            def _():
                settled(qg.at[slot, :, place], relay_send.at[slot, place])

            @pl.when(jnp.logical_not(jnp.logical_and(reach == 0, core == turn)))
            def _():
                settled(dq_out.at[step, turn], out_send.at[0, slot, place])
                settled(dkv_out.at[slot, :, place], out_send.at[1, slot, place])

        return 0

    lax.fori_loop(0, steps, drain, 0)

    def receive(head, _):
        settled(grads.at[0, :, columns(head)], out_recv.at[0, head])
        settled(grads.at[pl.ds(1, 2), :, columns(head)], out_recv.at[1, head])
        return 0

    lax.fori_loop(0, HEADS, receive, 0)


def settle_kernel(grads, *refs):
    copies = [pltpu.make_async_copy(grads.at[i], refs[i], refs[3].at[i]) for i in range(3)]
    for copy in copies:
        copy.start()
    for copy in copies:
        copy.wait()


def settle(grads):
    anywhere = pl.BlockSpec(memory_space=pl.ANY)
    return pl.pallas_call(
        settle_kernel,
        out_shape=[pltpu.HBM(grads.shape[1:], grads.dtype)] * 3,
        in_specs=[anywhere],
        out_specs=[anywhere] * 3,
        scratch_shapes=[pltpu.SemaphoreType.DMA((3,))],
    )(pltpu.with_memory_space_constraint(grads, pltpu.VMEM))


def half_body(queries, keys, values, out_grad, tile_lists):
    shape = (TILE, HEADS * DH)
    blocks = [array.reshape(shape) for array in (queries, keys, values, out_grad)]
    anywhere = pl.BlockSpec(memory_space=pl.ANY)
    side_rows = SIDE_TILES * TILE
    low = jnp.bfloat16
    full = jnp.float32
    dma = pltpu.SemaphoreType.DMA
    grads = pl.pallas_call(
        half_kernel,
        out_shape=pltpu.VMEM((3,) + shape, low),
        in_specs=[anywhere] * 5,
        out_specs=anywhere,
        scratch_shapes=[
            pltpu.VMEM((4,) + shape, low),
            pltpu.VMEM((INNER_SLOTS, 2, 2 * SIDE_TILES, TILE, DH), low),
            pltpu.VMEM((INNER_SLOTS, 2, SIDE_TILES, TILE, DH), low),
            pltpu.VMEM((TENSOR_DEVICES,) + tile_lists.shape, jnp.int32),
            pltpu.VMEM((CHIPS, SIDE_TILES, WIDE), full),
            pltpu.VMEM((INNER_SLOTS, CHIPS, DH, 2 * TILE), low),
            pltpu.VMEM((BUFFERS, side_rows, WIDE), full),
            pltpu.VMEM((BUFFERS, side_rows, WIDE), full),
            pltpu.VMEM((MAX_STEPS, 8, TILE), full),
            pltpu.VMEM((MAX_STEPS, 8, TILE), full),
            pltpu.VMEM((BUFFERS, 1, WIDE), full),
            pltpu.VMEM((side_rows, DH), full),
            pltpu.VMEM((side_rows, DH), full),
            pltpu.VMEM((KEPT, DH, 2 * TILE), full),
            pltpu.VMEM((MAX_STEPS, DH, 2 * TILE), low),
            pltpu.VMEM((MAX_STEPS, DH, 2 * TILE), low),
            pltpu.VMEM((MAX_STEPS, 2, TILE, DH), low),
            pltpu.VMEM((INNER_SLOTS, 2, SIDE_TILES, TILE, DH), low),
            dma((4 * len(SEND_ORDER),)),
            dma((2, INNER_SLOTS, SIDE_TILES)),
            dma((INNER_SLOTS, SIDE_TILES)),
            dma((INNER_SLOTS, SIDE_TILES)),
            dma((MAX_STEPS,)),
            dma((MAX_STEPS,)),
            dma((MAX_STEPS,)),
            dma((MAX_STEPS,)),
            dma((2, INNER_SLOTS, SIDE_TILES)),
            dma((2, HEADS)),
            dma((1,)),
            dma((TENSOR_DEVICES,)),
            dma((5,)),
        ],
        compiler_params=pltpu.CompilerParams(
            collective_id=0, has_side_effects=True, vmem_limit_bytes=60 * 1024 * 1024
        ),
    )(*blocks, tile_lists)
    return tuple(grad.reshape(queries.shape) for grad in settle(grads))


def body(queries, keys, values, out_grad, tile_lists):
    grid = (lax.axis_size("seq"), lax.axis_size("tensor"))
    if grid == (SEQ_DEVICES, TENSOR_DEVICES) and queries.shape == (1, TILE, HEADS * DH):
        return half_body(queries, keys, values, out_grad, tile_lists)
    return regrouped_body(queries, keys, values, out_grad, tile_lists)


def solution(mesh):
    return jax.shard_map(
        body,
        mesh=mesh,
        in_specs=(
            P(("groups", "tensor"), "seq", None),
            P(("groups", "tensor"), "seq", None),
            P(("groups", "tensor"), "seq", None),
            P(("groups", "tensor"), "seq", None),
            P(("groups", "tensor"), None),
        ),
        out_specs=(
            P(("groups", "tensor"), "seq", None),
            P(("groups", "tensor"), "seq", None),
            P(("groups", "tensor"), "seq", None),
        ),
        check_vma=False,
    )
```

```python
import functools
import math

import jax
import jax.numpy as jnp
from jax import lax
from jax.experimental import pallas as pl
from jax.experimental.pallas import tpu as pltpu
from jax.sharding import PartitionSpec as P

HEADS = 16
DH = 128
TILE = 128
RADIUS = 8
WIN = 12


block_tiles = 4


def padded_2(block, sides, width):
    for axis, dim in sides:
        count = lax.axis_size(axis)
        forward = [(i, i + 1) for i in range(count - 1)]
        backward = [(target, source) for source, target in forward]
        low = lax.ppermute(
            lax.slice_in_dim(block, block.shape[dim] - width, None, axis=dim), axis, forward
        )
        high = lax.ppermute(lax.slice_in_dim(block, 0, width, axis=dim), axis, backward)
        block = jnp.concatenate([low, block, high], axis=dim)
    return block


def key_rims(key_rows, value_rows):
    joined = jnp.concatenate([key_rows, value_rows], 1)
    return padded_2(joined, (("tensor", 0),), RADIUS * TILE)


def finish_rims(grads_ext, segment, local_width):
    rim_rows = RADIUS * TILE
    outer_rows = jnp.concatenate([grads_ext[:rim_rows], grads_ext[-rim_rows:]], 0)
    arrived = padded_2(outer_rows, (("tensor", 0),), rim_rows)
    own_rows = grads_ext[rim_rows : rim_rows + segment]
    own_rows = own_rows.at[:rim_rows].add(arrived[:rim_rows])
    own_rows = own_rows.at[segment - rim_rows :].add(arrived[3 * rim_rows :])
    own_rows = own_rows.astype(jnp.bfloat16)
    return (own_rows[:, :local_width], own_rows[:, local_width:])


def regrouped_body(queries, keys, values, out_grad, tile_lists):
    span_rows = queries.shape[1]
    feature_count = queries.shape[2]
    seq_count = lax.axis_size("seq")
    heads_here = HEADS // seq_count
    local_width = heads_here * DH
    score_scale = 1.0 / math.sqrt(DH)
    query_tokens = queries.reshape(span_rows, feature_count)
    key_tokens = keys.reshape(span_rows, feature_count)
    value_tokens = values.reshape(span_rows, feature_count)
    grad_tokens = out_grad.reshape(span_rows, feature_count)
    query_rows, key_rows, value_rows, grad_rows = (
        lax.all_to_all(query_tokens, "seq", split_axis=1, concat_axis=0, tiled=True),
        lax.all_to_all(key_tokens, "seq", split_axis=1, concat_axis=0, tiled=True),
        lax.all_to_all(value_tokens, "seq", split_axis=1, concat_axis=0, tiled=True),
        lax.all_to_all(grad_tokens, "seq", split_axis=1, concat_axis=0, tiled=True),
    )
    padded = key_rims(key_rows, value_rows)
    segment = query_rows.shape[0]
    seg_tiles = segment // TILE
    ext_tiles = seg_tiles + 2 * RADIUS
    block_count = seg_tiles // block_tiles
    first_tile = lax.axis_index("tensor") * seg_tiles - RADIUS
    kv_tiles = padded.reshape(ext_tiles, TILE, 2 * local_width)
    query_blocks = query_rows.reshape(block_count, block_tiles, TILE, heads_here, DH)
    grad_blocks = grad_rows.reshape(block_count, block_tiles, TILE, heads_here, DH)
    list_blocks = tile_lists.reshape(block_count, block_tiles, WIN)

    def attend_block(totals, inputs):
        query_block, grad_block, tile_rows = inputs
        present = tile_rows >= 0
        local_tile = jnp.clip(tile_rows - first_tile, 0, ext_tiles - 1)
        picked = jnp.concatenate(
            [
                lax.dynamic_slice_in_dim(kv_tiles, local_tile[row, entry], 1, 0)
                for row in range(block_tiles)
                for entry in range(WIN)
            ],
            0,
        ).reshape(block_tiles, WIN * TILE, 2, heads_here, DH)
        key_sel = picked[:, :, 0]
        value_sel = picked[:, :, 1]
        scores = (
            jnp.einsum("gthd,gkhd->ghtk", query_block, key_sel, preferred_element_type=jnp.float32)
            * score_scale
        )
        live_keys = jnp.repeat(present, TILE, axis=1)
        scores = jnp.where(live_keys[:, None, None, :], scores, -1e30)
        row_max = jnp.max(scores, axis=3, keepdims=True)
        weights = jnp.exp(scores - row_max)
        weights = weights / jnp.sum(weights, axis=3, keepdims=True)
        weights_b = weights.astype(jnp.bfloat16)
        recomputed = jnp.einsum(
            "ghtk,gkhd->gthd", weights_b, value_sel, preferred_element_type=jnp.float32
        )
        delta = jnp.sum(grad_block.astype(jnp.float32) * recomputed, axis=3)
        prob_grad = jnp.einsum(
            "gthd,gkhd->ghtk", grad_block, value_sel, preferred_element_type=jnp.float32
        )
        score_grad = (
            weights * (prob_grad - jnp.transpose(delta, (0, 2, 1))[..., None]) * score_scale
        ).astype(jnp.bfloat16)
        query_part = jnp.einsum(
            "ghtk,gkhd->gthd", score_grad, key_sel, preferred_element_type=jnp.float32
        ).astype(jnp.bfloat16)
        key_part = jnp.einsum(
            "ghtk,gthd->gkhd", score_grad, query_block, preferred_element_type=jnp.float32
        )
        value_part = jnp.einsum(
            "ghtk,gthd->gkhd", weights_b, grad_block, preferred_element_type=jnp.float32
        )
        key_terms = jnp.concatenate([key_part, value_part], 2).reshape(
            block_tiles, WIN, TILE, 2 * local_width
        )
        totals = totals.at[local_tile].add(key_terms)
        return (totals, query_part)

    initial = jnp.zeros((ext_tiles, TILE, 2 * local_width), jnp.float32)
    grads_ext, query_parts = lax.scan(
        attend_block, initial, (query_blocks, grad_blocks, list_blocks)
    )
    query_grad = query_parts.reshape(segment, local_width)
    grads_ext = grads_ext.reshape(ext_tiles * TILE, 2 * local_width)
    query_back = lax.all_to_all(query_grad, "seq", split_axis=0, concat_axis=1, tiled=True)
    key_grad, value_grad = finish_rims(grads_ext, segment, local_width)
    key_back, value_back = (
        lax.all_to_all(key_grad, "seq", split_axis=0, concat_axis=1, tiled=True),
        lax.all_to_all(value_grad, "seq", split_axis=0, concat_axis=1, tiled=True),
    )
    out_shape = queries.shape
    return (
        query_back.reshape(out_shape),
        key_back.reshape(out_shape),
        value_back.reshape(out_shape),
    )


def partner_order(seq_count, tensor_count):
    order = []
    for step in range(seq_count):
        reach = (seq_count // 2 + ((step + 1) // 2) * (1 - 2 * (step % 2))) % seq_count
        for turn in range(tensor_count):
            if reach or turn:
                order.append((reach, turn))
    return order[::-1]


def head_kernel(
    seq_count,
    tensor_count,
    q_hbm,
    k_hbm,
    v_hbm,
    g_hbm,
    lists_hbm,
    dq_hbm,
    dk_hbm,
    dv_hbm,
    qk_all,
    v_all,
    g_all,
    lists_all,
    bias,
    probs,
    prob_grad,
    key_t,
    dv_sum,
    dk_sum,
    dq_out,
    dk_out,
    dv_out,
    staged,
    in_send,
    in_recv,
    out_send,
    out_recv,
    list_send,
    list_recv,
    local_sem,
):
    seq_here = lax.axis_index("seq")
    tensor_here = lax.axis_index("tensor")
    me = tensor_here * seq_count + seq_here
    tiles = seq_count * tensor_count
    pairs = tiles // 2
    score_scale = 1.0 / math.sqrt(DH)
    partners = []
    for reach, turn in partner_order(seq_count, tensor_count):
        seq_there = lax.rem(seq_here + reach, seq_count)
        tensor_there = lax.rem(tensor_here + turn, tensor_count)
        partners.append((seq_there, tensor_there, tensor_there * seq_count + seq_there))

    def columns(index):
        return pl.ds(pl.multiple_of(index * DH, DH), DH)

    def remote(src, dst, send, recv, seq_there, tensor_there):
        return pltpu.make_async_remote_copy(
            src_ref=src,
            dst_ref=dst,
            send_sem=send,
            recv_sem=recv,
            device_id={"seq": seq_there, "tensor": tensor_there},
            device_id_type=pl.DeviceIdType.MESH,
        )

    staging = [
        pltpu.make_async_copy(src, staged.at[which], local_sem.at[8 + which])
        for which, src in enumerate((q_hbm, k_hbm, g_hbm, v_hbm))
    ]
    q_all, k_all = qk_all.at[0], qk_all.at[1]
    incoming = {
        0: (lambda cols: staged.at[pl.ds(0, 2), :, cols], lambda slot: qk_all.at[:, slot]),
        2: (lambda cols: staged.at[2, :, cols], lambda slot: g_all.at[slot]),
        3: (lambda cols: staged.at[3, :, cols], lambda slot: v_all.at[slot]),
    }
    outgoing = ((dv_out, dv_hbm), (dq_out, dq_hbm), (dk_out, dk_hbm))

    def in_copy(which, seq_there, tensor_there, there):
        src, dst = incoming[which]
        return remote(
            src(columns(there)),
            dst(me),
            in_send.at[which, there],
            in_recv.at[which, me],
            seq_there,
            tensor_there,
        )

    def in_wait(which, seq_there, tensor_there, there):
        src, dst = incoming[which]
        remote(
            src(columns(there)),
            dst(there),
            in_send.at[which, there],
            in_recv.at[which, there],
            seq_there,
            tensor_there,
        ).wait()

    def in_local(which):
        src, dst = incoming[which]
        return pltpu.make_async_copy(src(columns(me)), dst(me), local_sem.at[which])

    def out_copy(which, seq_there, tensor_there, there):
        src, dst = outgoing[which]
        return remote(
            src.at[there],
            dst.at[:, columns(me)],
            out_send.at[which, there],
            out_recv.at[which, me],
            seq_there,
            tensor_there,
        )

    def out_wait(which, seq_there, tensor_there, there):
        src, dst = outgoing[which]
        remote(
            src.at[there],
            dst.at[:, columns(there)],
            out_send.at[which, there],
            out_recv.at[which, there],
            seq_there,
            tensor_there,
        ).wait()

    def out_local(which):
        src, dst = outgoing[which]
        return pltpu.make_async_copy(src.at[me], dst.at[:, columns(me)], local_sem.at[4 + which])

    for copy in staging:
        copy.start()
    own_list = pltpu.make_async_copy(lists_hbm, lists_all.at[tensor_here], local_sem.at[7])
    own_list.start()

    barrier = pltpu.get_barrier_semaphore()
    for seq_there, tensor_there, _ in partners:
        pl.semaphore_signal(
            barrier,
            inc=1,
            device_id={"seq": seq_there, "tensor": tensor_there},
            device_id_type=pl.DeviceIdType.MESH,
        )
    pl.semaphore_wait(barrier, len(partners))

    def list_copy(turn, slot):
        return remote(
            lists_hbm,
            lists_all.at[slot],
            list_send.at[turn],
            list_recv.at[slot],
            seq_here,
            lax.rem(tensor_here + turn, tensor_count),
        )

    for turn in range(1, tensor_count):
        list_copy(turn, tensor_here).start()
    for group in ((0, 1), (2,), (3,)):
        for which in group:
            staging[which].wait()
        in_local(group[0]).start()
        for partner in partners:
            in_copy(group[0], *partner).start()

    own_list.wait()
    for turn in range(1, tensor_count):
        list_copy(turn, lax.rem(tensor_here + turn, tensor_count)).wait()
    tile_ids = lax.broadcasted_iota(jnp.int32, (tiles, TILE), 0)
    for tile in range(tiles):
        row = lists_all[tile // seq_count, tile % seq_count : tile % seq_count + 1, :]
        miss = jnp.full((tiles, TILE), -1e30, jnp.float32)
        for entry in range(WIN):
            miss = jnp.where(row[:, entry : entry + 1] == tile_ids, 0.0, miss)
        half = (tile % 2) * TILE
        bias[tile // 2, :, half : half + TILE] = miss

    dv_sum[...] = jnp.zeros_like(dv_sum)
    dk_sum[...] = jnp.zeros_like(dk_sum)

    in_local(0).wait()
    for partner in partners:
        in_wait(0, *partner)

    def pair_rows(ref, index):
        return ref[pl.ds(2 * index, 2)].reshape(2 * TILE, DH)

    def turned(block):
        return block.astype(jnp.float32).T.astype(jnp.bfloat16)

    def key_rows(index):
        return pl.ds(index * 2 * TILE, 2 * TILE)

    def fold(block, op):
        return op(block.reshape(2 * TILE // 8, 8, 2 * TILE), axis=0)

    def score_pair(pair, _):
        query_t = turned(pair_rows(q_all, pair))
        key_t[pair] = turned(pair_rows(k_all, pair))
        top = jnp.full((8, 2 * TILE), -3e38, jnp.float32)
        for chunk in range(pairs):
            scores = (
                jnp.dot(pair_rows(k_all, chunk), query_t, preferred_element_type=jnp.float32)
                * score_scale
            )
            scores = jnp.concatenate(
                [
                    scores[:TILE] + bias[pair, 2 * chunk : 2 * chunk + 1, :],
                    scores[TILE:] + bias[pair, 2 * chunk + 1 : 2 * chunk + 2, :],
                ],
                axis=0,
            )
            probs[pair, key_rows(chunk), :] = scores
            top = jnp.maximum(top, fold(scores, jnp.max))
        top = jnp.max(top, axis=0, keepdims=True)
        total = jnp.zeros((8, 2 * TILE), jnp.float32)
        for chunk in range(pairs):
            weights = jnp.exp(probs[pair, key_rows(chunk), :] - top)
            probs[pair, key_rows(chunk), :] = weights
            total = total + fold(weights, jnp.sum)
        inverse = 1.0 / jnp.sum(total, axis=0, keepdims=True)
        for chunk in range(pairs):
            probs[pair, key_rows(chunk), :] = probs[pair, key_rows(chunk), :] * inverse
        return 0

    lax.fori_loop(0, pairs, score_pair, 0)

    in_local(2).wait()
    for partner in partners:
        in_wait(2, *partner)

    def value_pair(pair, _):
        grad_pair = pair_rows(g_all, pair)
        for chunk in range(pairs):
            dv_sum[key_rows(chunk), :] += jnp.dot(
                probs[pair, key_rows(chunk), :].astype(jnp.bfloat16),
                grad_pair,
                preferred_element_type=jnp.float32,
            )
        return 0

    lax.fori_loop(0, pairs, value_pair, 0)
    dv_out[...] = dv_sum[...].astype(jnp.bfloat16).reshape(dv_out.shape)
    for partner in partners:
        out_copy(0, *partner).start()
    out_local(0).start()

    in_local(3).wait()
    for partner in partners:
        in_wait(3, *partner)

    def grad_pair_step(pair, _):
        query_pair = pair_rows(q_all, pair)
        grad_t = turned(pair_rows(g_all, pair))
        delta = jnp.zeros((8, 2 * TILE), jnp.float32)
        for chunk in range(pairs):
            product = jnp.dot(pair_rows(v_all, chunk), grad_t, preferred_element_type=jnp.float32)
            prob_grad[key_rows(chunk), :] = product
            rounded = probs[pair, key_rows(chunk), :].astype(jnp.bfloat16).astype(jnp.float32)
            delta = delta + fold(rounded * product, jnp.sum)
        delta = jnp.sum(delta, axis=0, keepdims=True)
        query_sum = jnp.zeros((DH, 2 * TILE), jnp.float32)
        for chunk in range(pairs):
            score_grad = (
                probs[pair, key_rows(chunk), :]
                * (prob_grad[key_rows(chunk), :] - delta)
                * score_scale
            ).astype(jnp.bfloat16)
            dk_sum[key_rows(chunk), :] += jnp.dot(
                score_grad, query_pair, preferred_element_type=jnp.float32
            )
            query_sum = query_sum + jnp.dot(
                key_t[chunk], score_grad, preferred_element_type=jnp.float32
            )
        dq_out[pl.ds(2 * pair, 2)] = query_sum.T.astype(jnp.bfloat16).reshape(2, TILE, DH)
        for side in range(2):
            there = 2 * pair + side

            @pl.when(there != me)
            def _():
                out_copy(1, lax.rem(there, seq_count), there // seq_count, there).start()

        return 0

    lax.fori_loop(0, pairs, grad_pair_step, 0)
    dk_out[...] = dk_sum[...].astype(jnp.bfloat16).reshape(dk_out.shape)
    for partner in partners:
        out_copy(2, *partner).start()
    out_local(1).start()
    out_local(2).start()

    for which in range(3):
        out_local(which).wait()
        for partner in partners:
            out_wait(which, *partner)


def settle_kernel(*refs):
    copies = [
        pltpu.make_async_copy(src, dst, refs[6].at[i])
        for i, (src, dst) in enumerate(zip(refs[:3], refs[3:6]))
    ]
    for copy in copies:
        copy.start()
    for copy in copies:
        copy.wait()


def settle(grads):
    anywhere = pl.BlockSpec(memory_space=pl.ANY)
    return pl.pallas_call(
        settle_kernel,
        out_shape=[pltpu.HBM(grad.shape, grad.dtype) for grad in grads],
        in_specs=[anywhere] * 3,
        out_specs=[anywhere] * 3,
        scratch_shapes=[pltpu.SemaphoreType.DMA((3,))],
    )(*[pltpu.with_memory_space_constraint(grad, pltpu.VMEM) for grad in grads])


def head_body(queries, keys, values, out_grad, tile_lists):
    seq_count = lax.axis_size("seq")
    tensor_count = lax.axis_size("tensor")
    tiles = seq_count * tensor_count
    pairs = tiles // 2
    shape = (TILE, HEADS * DH)
    blocks = [array.reshape(shape) for array in (queries, keys, values, out_grad)]
    anywhere = pl.BlockSpec(memory_space=pl.ANY)
    per_tile = pltpu.VMEM((tiles, TILE, DH), jnp.bfloat16)
    grads = pl.pallas_call(
        functools.partial(head_kernel, seq_count, tensor_count),
        out_shape=[pltpu.VMEM(shape, jnp.bfloat16)] * 3,
        in_specs=[anywhere] * 5,
        out_specs=[anywhere] * 3,
        scratch_shapes=[
            pltpu.VMEM((2, tiles, TILE, DH), jnp.bfloat16),
            per_tile,
            per_tile,
            pltpu.VMEM((tensor_count,) + tile_lists.shape, jnp.int32),
            pltpu.VMEM((pairs, tiles, 2 * TILE), jnp.float32),
            pltpu.VMEM((pairs, tiles * TILE, 2 * TILE), jnp.float32),
            pltpu.VMEM((tiles * TILE, 2 * TILE), jnp.float32),
            pltpu.VMEM((pairs, DH, 2 * TILE), jnp.bfloat16),
            pltpu.VMEM((tiles * TILE, DH), jnp.float32),
            pltpu.VMEM((tiles * TILE, DH), jnp.float32),
            per_tile,
            per_tile,
            per_tile,
            pltpu.VMEM((4,) + shape, jnp.bfloat16),
            pltpu.SemaphoreType.DMA((4, tiles)),
            pltpu.SemaphoreType.DMA((4, tiles)),
            pltpu.SemaphoreType.DMA((3, tiles)),
            pltpu.SemaphoreType.DMA((3, tiles)),
            pltpu.SemaphoreType.DMA((tensor_count,)),
            pltpu.SemaphoreType.DMA((tensor_count,)),
            pltpu.SemaphoreType.DMA((12,)),
        ],
        compiler_params=pltpu.CompilerParams(
            collective_id=0, has_side_effects=True, vmem_limit_bytes=60 * 1024 * 1024
        ),
    )(*blocks, tile_lists)
    return tuple(grad.reshape(queries.shape) for grad in settle(grads))


def body(queries, keys, values, out_grad, tile_lists):
    devices = lax.axis_size("seq") * lax.axis_size("tensor")
    one_head_one_tile = devices == HEADS and queries.shape[:2] == (1, TILE)
    if one_head_one_tile and queries.shape[2] == HEADS * DH:
        return head_body(queries, keys, values, out_grad, tile_lists)
    return regrouped_body(queries, keys, values, out_grad, tile_lists)


def solution(mesh):
    return jax.shard_map(
        body,
        mesh=mesh,
        in_specs=(
            P(("groups", "tensor"), "seq", None),
            P(("groups", "tensor"), "seq", None),
            P(("groups", "tensor"), "seq", None),
            P(("groups", "tensor"), "seq", None),
            P(("groups", "tensor"), None),
        ),
        out_specs=(
            P(("groups", "tensor"), "seq", None),
            P(("groups", "tensor"), "seq", None),
            P(("groups", "tensor"), "seq", None),
        ),
        check_vma=False,
    )
```

```python
import functools
import math

import jax
import jax.numpy as jnp
from jax import lax
from jax.experimental import pallas as pl
from jax.experimental.pallas import tpu as pltpu
from jax.sharding import PartitionSpec as P

HEADS = 16
DH = 128
TILE = 128
RADIUS = 8
WIN = 12


block_tiles = 4


def padded_2(block, sides, width):
    for axis, dim in sides:
        count = lax.axis_size(axis)
        forward = [(i, i + 1) for i in range(count - 1)]
        backward = [(target, source) for source, target in forward]
        low = lax.ppermute(
            lax.slice_in_dim(block, block.shape[dim] - width, None, axis=dim), axis, forward
        )
        high = lax.ppermute(lax.slice_in_dim(block, 0, width, axis=dim), axis, backward)
        block = jnp.concatenate([low, block, high], axis=dim)
    return block


def key_rims(key_rows, value_rows):
    joined = jnp.concatenate([key_rows, value_rows], 1)
    return padded_2(joined, (("tensor", 0),), RADIUS * TILE)


def finish_rims(grads_ext, segment, local_width):
    rim_rows = RADIUS * TILE
    outer_rows = jnp.concatenate([grads_ext[:rim_rows], grads_ext[-rim_rows:]], 0)
    arrived = padded_2(outer_rows, (("tensor", 0),), rim_rows)
    own_rows = grads_ext[rim_rows : rim_rows + segment]
    own_rows = own_rows.at[:rim_rows].add(arrived[:rim_rows])
    own_rows = own_rows.at[segment - rim_rows :].add(arrived[3 * rim_rows :])
    own_rows = own_rows.astype(jnp.bfloat16)
    return (own_rows[:, :local_width], own_rows[:, local_width:])


def regrouped_body(queries, keys, values, out_grad, tile_lists):
    span_rows = queries.shape[1]
    feature_count = queries.shape[2]
    seq_count = lax.axis_size("seq")
    heads_here = HEADS // seq_count
    local_width = heads_here * DH
    score_scale = 1.0 / math.sqrt(DH)
    query_tokens = queries.reshape(span_rows, feature_count)
    key_tokens = keys.reshape(span_rows, feature_count)
    value_tokens = values.reshape(span_rows, feature_count)
    grad_tokens = out_grad.reshape(span_rows, feature_count)
    query_rows, key_rows, value_rows, grad_rows = (
        lax.all_to_all(query_tokens, "seq", split_axis=1, concat_axis=0, tiled=True),
        lax.all_to_all(key_tokens, "seq", split_axis=1, concat_axis=0, tiled=True),
        lax.all_to_all(value_tokens, "seq", split_axis=1, concat_axis=0, tiled=True),
        lax.all_to_all(grad_tokens, "seq", split_axis=1, concat_axis=0, tiled=True),
    )
    padded = key_rims(key_rows, value_rows)
    segment = query_rows.shape[0]
    seg_tiles = segment // TILE
    ext_tiles = seg_tiles + 2 * RADIUS
    block_count = seg_tiles // block_tiles
    first_tile = lax.axis_index("tensor") * seg_tiles - RADIUS
    kv_tiles = padded.reshape(ext_tiles, TILE, 2 * local_width)
    query_blocks = query_rows.reshape(block_count, block_tiles, TILE, heads_here, DH)
    grad_blocks = grad_rows.reshape(block_count, block_tiles, TILE, heads_here, DH)
    list_blocks = tile_lists.reshape(block_count, block_tiles, WIN)

    def attend_block(totals, inputs):
        query_block, grad_block, tile_rows = inputs
        present = tile_rows >= 0
        local_tile = jnp.clip(tile_rows - first_tile, 0, ext_tiles - 1)
        picked = jnp.concatenate(
            [
                lax.dynamic_slice_in_dim(kv_tiles, local_tile[row, entry], 1, 0)
                for row in range(block_tiles)
                for entry in range(WIN)
            ],
            0,
        ).reshape(block_tiles, WIN * TILE, 2, heads_here, DH)
        key_sel = picked[:, :, 0]
        value_sel = picked[:, :, 1]
        scores = (
            jnp.einsum("gthd,gkhd->ghtk", query_block, key_sel, preferred_element_type=jnp.float32)
            * score_scale
        )
        live_keys = jnp.repeat(present, TILE, axis=1)
        scores = jnp.where(live_keys[:, None, None, :], scores, -1e30)
        row_max = jnp.max(scores, axis=3, keepdims=True)
        weights = jnp.exp(scores - row_max)
        weights = weights / jnp.sum(weights, axis=3, keepdims=True)
        weights_b = weights.astype(jnp.bfloat16)
        recomputed = jnp.einsum(
            "ghtk,gkhd->gthd", weights_b, value_sel, preferred_element_type=jnp.float32
        )
        delta = jnp.sum(grad_block.astype(jnp.float32) * recomputed, axis=3)
        prob_grad = jnp.einsum(
            "gthd,gkhd->ghtk", grad_block, value_sel, preferred_element_type=jnp.float32
        )
        score_grad = (
            weights * (prob_grad - jnp.transpose(delta, (0, 2, 1))[..., None]) * score_scale
        ).astype(jnp.bfloat16)
        query_part = jnp.einsum(
            "ghtk,gkhd->gthd", score_grad, key_sel, preferred_element_type=jnp.float32
        ).astype(jnp.bfloat16)
        key_part = jnp.einsum(
            "ghtk,gthd->gkhd", score_grad, query_block, preferred_element_type=jnp.float32
        )
        value_part = jnp.einsum(
            "ghtk,gthd->gkhd", weights_b, grad_block, preferred_element_type=jnp.float32
        )
        key_terms = jnp.concatenate([key_part, value_part], 2).reshape(
            block_tiles, WIN, TILE, 2 * local_width
        )
        totals = totals.at[local_tile].add(key_terms)
        return (totals, query_part)

    initial = jnp.zeros((ext_tiles, TILE, 2 * local_width), jnp.float32)
    grads_ext, query_parts = lax.scan(
        attend_block, initial, (query_blocks, grad_blocks, list_blocks)
    )
    query_grad = query_parts.reshape(segment, local_width)
    grads_ext = grads_ext.reshape(ext_tiles * TILE, 2 * local_width)
    query_back = lax.all_to_all(query_grad, "seq", split_axis=0, concat_axis=1, tiled=True)
    key_grad, value_grad = finish_rims(grads_ext, segment, local_width)
    key_back, value_back = (
        lax.all_to_all(key_grad, "seq", split_axis=0, concat_axis=1, tiled=True),
        lax.all_to_all(value_grad, "seq", split_axis=0, concat_axis=1, tiled=True),
    )
    out_shape = queries.shape
    return (
        query_back.reshape(out_shape),
        key_back.reshape(out_shape),
        value_back.reshape(out_shape),
    )


def partner_order(seq_count, tensor_count):
    half = seq_count // 2
    order = []
    for far in (1, 0):
        for reach in range(half):
            for turn in range(tensor_count):
                if far or reach or turn:
                    order.append((far, reach, turn))
    return order


def head_kernel(
    seq_count,
    tensor_count,
    q_hbm,
    k_hbm,
    v_hbm,
    g_hbm,
    lists_hbm,
    dq_hbm,
    dk_hbm,
    dv_hbm,
    qk_all,
    v_all,
    g_all,
    lists_all,
    bias,
    probs,
    prob_grad,
    key_t,
    dv_sum,
    dk_sum,
    dq_out,
    dk_out,
    dv_out,
    staged,
    in_send,
    in_recv,
    out_send,
    out_recv,
    list_send,
    list_recv,
    local_sem,
):
    seq_here = lax.axis_index("seq")
    tensor_here = lax.axis_index("tensor")
    me = tensor_here * seq_count + seq_here
    tiles = seq_count * tensor_count
    pairs = tiles // 2
    score_scale = 1.0 / math.sqrt(DH)
    partners = []
    half = seq_count // 2
    for far, reach, turn in partner_order(seq_count, tensor_count):
        seq_there = half * lax.rem(seq_here // half + far, 2) + lax.rem(seq_here + reach, half)
        tensor_there = lax.rem(tensor_here + turn, tensor_count)
        partners.append((seq_there, tensor_there, tensor_there * seq_count + seq_there))

    def columns(index):
        return pl.ds(pl.multiple_of(index * DH, DH), DH)

    def remote(src, dst, send, recv, seq_there, tensor_there):
        return pltpu.make_async_remote_copy(
            src_ref=src,
            dst_ref=dst,
            send_sem=send,
            recv_sem=recv,
            device_id={"seq": seq_there, "tensor": tensor_there},
            device_id_type=pl.DeviceIdType.MESH,
        )

    staging = [
        pltpu.make_async_copy(src, staged.at[which], local_sem.at[8 + which])
        for which, src in enumerate((q_hbm, k_hbm, g_hbm, v_hbm))
    ]
    q_all, k_all = qk_all.at[0], qk_all.at[1]
    incoming = {
        0: (lambda cols: staged.at[pl.ds(0, 2), :, cols], lambda slot: qk_all.at[:, slot]),
        2: (lambda cols: staged.at[2, :, cols], lambda slot: g_all.at[slot]),
        3: (lambda cols: staged.at[3, :, cols], lambda slot: v_all.at[slot]),
    }
    outgoing = ((dv_out, dv_hbm), (dq_out, dq_hbm), (dk_out, dk_hbm))

    def in_copy(which, seq_there, tensor_there, there):
        src, dst = incoming[which]
        return remote(
            src(columns(there)),
            dst(me),
            in_send.at[which, there],
            in_recv.at[which, me],
            seq_there,
            tensor_there,
        )

    def in_wait(which, seq_there, tensor_there, there):
        src, dst = incoming[which]
        remote(
            src(columns(there)),
            dst(there),
            in_send.at[which, there],
            in_recv.at[which, there],
            seq_there,
            tensor_there,
        ).wait()

    def in_local(which):
        src, dst = incoming[which]
        return pltpu.make_async_copy(src(columns(me)), dst(me), local_sem.at[which])

    def out_copy(which, seq_there, tensor_there, there):
        src, dst = outgoing[which]
        return remote(
            src.at[there],
            dst.at[:, columns(me)],
            out_send.at[which, there],
            out_recv.at[which, me],
            seq_there,
            tensor_there,
        )

    def out_wait(which, seq_there, tensor_there, there):
        src, dst = outgoing[which]
        remote(
            src.at[there],
            dst.at[:, columns(there)],
            out_send.at[which, there],
            out_recv.at[which, there],
            seq_there,
            tensor_there,
        ).wait()

    def out_local(which):
        src, dst = outgoing[which]
        return pltpu.make_async_copy(src.at[me], dst.at[:, columns(me)], local_sem.at[4 + which])

    for copy in staging:
        copy.start()
    own_list = pltpu.make_async_copy(lists_hbm, lists_all.at[tensor_here], local_sem.at[7])
    own_list.start()

    barrier = pltpu.get_barrier_semaphore()
    for seq_there, tensor_there, _ in partners:
        pl.semaphore_signal(
            barrier,
            inc=1,
            device_id={"seq": seq_there, "tensor": tensor_there},
            device_id_type=pl.DeviceIdType.MESH,
        )
    pl.semaphore_wait(barrier, len(partners))

    def list_copy(turn, slot):
        return remote(
            lists_hbm,
            lists_all.at[slot],
            list_send.at[turn],
            list_recv.at[slot],
            seq_here,
            lax.rem(tensor_here + turn, tensor_count),
        )

    for turn in range(1, tensor_count):
        list_copy(turn, tensor_here).start()
    for group in ((0, 1), (2,), (3,)):
        for which in group:
            staging[which].wait()
        in_local(group[0]).start()
        for partner in partners:
            in_copy(group[0], *partner).start()

    own_list.wait()
    for turn in range(1, tensor_count):
        list_copy(turn, lax.rem(tensor_here + turn, tensor_count)).wait()
    tile_ids = lax.broadcasted_iota(jnp.int32, (tiles, TILE), 0)
    for tile in range(tiles):
        row = lists_all[tile // seq_count, tile % seq_count : tile % seq_count + 1, :]
        miss = jnp.full((tiles, TILE), -1e30, jnp.float32)
        for entry in range(WIN):
            miss = jnp.where(row[:, entry : entry + 1] == tile_ids, 0.0, miss)
        half = (tile % 2) * TILE
        bias[tile // 2, :, half : half + TILE] = miss

    dv_sum[...] = jnp.zeros_like(dv_sum)
    dk_sum[...] = jnp.zeros_like(dk_sum)

    in_local(0).wait()
    for partner in partners:
        in_wait(0, *partner)

    def pair_rows(ref, index):
        return ref[pl.ds(2 * index, 2)].reshape(2 * TILE, DH)

    def turned(block):
        return block.astype(jnp.float32).T.astype(jnp.bfloat16)

    def key_rows(index):
        return pl.ds(index * 2 * TILE, 2 * TILE)

    def fold(block, op):
        return op(block.reshape(2 * TILE // 8, 8, 2 * TILE), axis=0)

    def score_pair(pair, _):
        query_t = turned(pair_rows(q_all, pair))
        key_t[pair] = turned(pair_rows(k_all, pair))
        top = jnp.full((8, 2 * TILE), -3e38, jnp.float32)
        for chunk in range(pairs):
            scores = (
                jnp.dot(pair_rows(k_all, chunk), query_t, preferred_element_type=jnp.float32)
                * score_scale
            )
            scores = jnp.concatenate(
                [
                    scores[:TILE] + bias[pair, 2 * chunk : 2 * chunk + 1, :],
                    scores[TILE:] + bias[pair, 2 * chunk + 1 : 2 * chunk + 2, :],
                ],
                axis=0,
            )
            probs[pair, key_rows(chunk), :] = scores
            top = jnp.maximum(top, fold(scores, jnp.max))
        top = jnp.max(top, axis=0, keepdims=True)
        total = jnp.zeros((8, 2 * TILE), jnp.float32)
        for chunk in range(pairs):
            weights = jnp.exp(probs[pair, key_rows(chunk), :] - top)
            probs[pair, key_rows(chunk), :] = weights
            total = total + fold(weights, jnp.sum)
        inverse = 1.0 / jnp.sum(total, axis=0, keepdims=True)
        for chunk in range(pairs):
            probs[pair, key_rows(chunk), :] = probs[pair, key_rows(chunk), :] * inverse
        return 0

    lax.fori_loop(0, pairs, score_pair, 0)

    in_local(2).wait()
    for partner in partners:
        in_wait(2, *partner)

    def value_pair(pair, _):
        grad_pair = pair_rows(g_all, pair)
        for chunk in range(pairs):
            dv_sum[key_rows(chunk), :] += jnp.dot(
                probs[pair, key_rows(chunk), :].astype(jnp.bfloat16),
                grad_pair,
                preferred_element_type=jnp.float32,
            )
        return 0

    lax.fori_loop(0, pairs, value_pair, 0)
    dv_out[...] = dv_sum[...].astype(jnp.bfloat16).reshape(dv_out.shape)
    for partner in partners:
        out_copy(0, *partner).start()
    out_local(0).start()

    in_local(3).wait()
    for partner in partners:
        in_wait(3, *partner)

    def grad_pair_step(pair, _):
        query_pair = pair_rows(q_all, pair)
        grad_t = turned(pair_rows(g_all, pair))
        delta = jnp.zeros((8, 2 * TILE), jnp.float32)
        for chunk in range(pairs):
            product = jnp.dot(pair_rows(v_all, chunk), grad_t, preferred_element_type=jnp.float32)
            prob_grad[key_rows(chunk), :] = product
            rounded = probs[pair, key_rows(chunk), :].astype(jnp.bfloat16).astype(jnp.float32)
            delta = delta + fold(rounded * product, jnp.sum)
        delta = jnp.sum(delta, axis=0, keepdims=True)
        query_sum = jnp.zeros((DH, 2 * TILE), jnp.float32)
        for chunk in range(pairs):
            score_grad = (
                probs[pair, key_rows(chunk), :]
                * (prob_grad[key_rows(chunk), :] - delta)
                * score_scale
            ).astype(jnp.bfloat16)
            dk_sum[key_rows(chunk), :] += jnp.dot(
                score_grad, query_pair, preferred_element_type=jnp.float32
            )
            query_sum = query_sum + jnp.dot(
                key_t[chunk], score_grad, preferred_element_type=jnp.float32
            )
        dq_out[pl.ds(2 * pair, 2)] = query_sum.T.astype(jnp.bfloat16).reshape(2, TILE, DH)
        for side in range(2):
            there = 2 * pair + side

            @pl.when(there != me)
            def _():
                out_copy(1, lax.rem(there, seq_count), there // seq_count, there).start()

        return 0

    lax.fori_loop(0, pairs, grad_pair_step, 0)
    dk_out[...] = dk_sum[...].astype(jnp.bfloat16).reshape(dk_out.shape)
    for partner in partners:
        out_copy(2, *partner).start()
    out_local(1).start()
    out_local(2).start()

    for which in range(3):
        out_local(which).wait()
        for partner in partners:
            out_wait(which, *partner)


def settle_kernel(*refs):
    copies = [
        pltpu.make_async_copy(src, dst, refs[6].at[i])
        for i, (src, dst) in enumerate(zip(refs[:3], refs[3:6]))
    ]
    for copy in copies:
        copy.start()
    for copy in copies:
        copy.wait()


def settle(grads):
    anywhere = pl.BlockSpec(memory_space=pl.ANY)
    return pl.pallas_call(
        settle_kernel,
        out_shape=[pltpu.HBM(grad.shape, grad.dtype) for grad in grads],
        in_specs=[anywhere] * 3,
        out_specs=[anywhere] * 3,
        scratch_shapes=[pltpu.SemaphoreType.DMA((3,))],
    )(*[pltpu.with_memory_space_constraint(grad, pltpu.VMEM) for grad in grads])


def head_body(queries, keys, values, out_grad, tile_lists):
    seq_count = lax.axis_size("seq")
    tensor_count = lax.axis_size("tensor")
    tiles = seq_count * tensor_count
    pairs = tiles // 2
    shape = (TILE, HEADS * DH)
    blocks = [array.reshape(shape) for array in (queries, keys, values, out_grad)]
    anywhere = pl.BlockSpec(memory_space=pl.ANY)
    per_tile = pltpu.VMEM((tiles, TILE, DH), jnp.bfloat16)
    grads = pl.pallas_call(
        functools.partial(head_kernel, seq_count, tensor_count),
        out_shape=[pltpu.VMEM(shape, jnp.bfloat16)] * 3,
        in_specs=[anywhere] * 5,
        out_specs=[anywhere] * 3,
        scratch_shapes=[
            pltpu.VMEM((2, tiles, TILE, DH), jnp.bfloat16),
            per_tile,
            per_tile,
            pltpu.VMEM((tensor_count,) + tile_lists.shape, jnp.int32),
            pltpu.VMEM((pairs, tiles, 2 * TILE), jnp.float32),
            pltpu.VMEM((pairs, tiles * TILE, 2 * TILE), jnp.float32),
            pltpu.VMEM((tiles * TILE, 2 * TILE), jnp.float32),
            pltpu.VMEM((pairs, DH, 2 * TILE), jnp.bfloat16),
            pltpu.VMEM((tiles * TILE, DH), jnp.float32),
            pltpu.VMEM((tiles * TILE, DH), jnp.float32),
            per_tile,
            per_tile,
            per_tile,
            pltpu.VMEM((4,) + shape, jnp.bfloat16),
            pltpu.SemaphoreType.DMA((4, tiles)),
            pltpu.SemaphoreType.DMA((4, tiles)),
            pltpu.SemaphoreType.DMA((3, tiles)),
            pltpu.SemaphoreType.DMA((3, tiles)),
            pltpu.SemaphoreType.DMA((tensor_count,)),
            pltpu.SemaphoreType.DMA((tensor_count,)),
            pltpu.SemaphoreType.DMA((12,)),
        ],
        compiler_params=pltpu.CompilerParams(
            collective_id=0, has_side_effects=True, vmem_limit_bytes=60 * 1024 * 1024
        ),
    )(*blocks, tile_lists)
    return tuple(grad.reshape(queries.shape) for grad in settle(grads))


def body(queries, keys, values, out_grad, tile_lists):
    devices = lax.axis_size("seq") * lax.axis_size("tensor")
    one_head_one_tile = devices == HEADS and lax.axis_size("seq") % 2 == 0 and queries.shape[:2] == (1, TILE)
    if one_head_one_tile and queries.shape[2] == HEADS * DH:
        return head_body(queries, keys, values, out_grad, tile_lists)
    return regrouped_body(queries, keys, values, out_grad, tile_lists)


def solution(mesh):
    return jax.shard_map(
        body,
        mesh=mesh,
        in_specs=(
            P(("groups", "tensor"), "seq", None),
            P(("groups", "tensor"), "seq", None),
            P(("groups", "tensor"), "seq", None),
            P(("groups", "tensor"), "seq", None),
            P(("groups", "tensor"), None),
        ),
        out_specs=(
            P(("groups", "tensor"), "seq", None),
            P(("groups", "tensor"), "seq", None),
            P(("groups", "tensor"), "seq", None),
        ),
        check_vma=False,
    )
```
